32 devices in a mesh: tm: 2 (over y), lon: 16 (over z, x, core).
Axes of the slice: x: 2, y: 2, z: 4, core: 2. Of those that a mesh axis runs over, the one named last changes fastest.
Arguments:
- first_guess: float32 [1, 8, 128, 128], P(None, 'tm', 'lon'), may hold values from -6 to 6
- observed: float32 [1, 8, 128, 128], P(None, 'tm', 'lon'), may hold values from -6 to 6
- obs_mask: int32 [1, 8, 128, 128], P(None, 'tm', 'lon'), may hold values 0 or 1
- land_mask: int32 [128, 128], P('lon'), may hold values 0 or 1
- enc_weight: float32 [32, 27], replicated, may hold values from -1.25 to 1.25
- enc_bias: float32 [32], replicated, may hold values from -0.5 to 0.5
- dec_weight: float32 [32, 27], replicated, may hold values from -0.21875 to 0.21875
- dec_bias: float32 [1], replicated, may hold values from -1 to 1
- gate_weight: bfloat16 [192, 441], replicated, may hold values from -0.25 to 0.25
- gate_bias: float32 [192], replicated, may hold values from -1 to 1
- out_weight: float32 [48], replicated, may hold values from -0.875 to 0.875
Outputs:
- analysis: float32 [1, 8, 128, 128], P(None, 'tm', 'lon')
The draws below stay inside these ranges and needn't reach their ends.
Inputs may be any that keep to these rules, and one draw needn't show every extreme that they name: `obs_mask`: 1 marks an observed cell on that day. `land_mask`: 1 marks a sea cell.
All inputs are finite; a program needn't handle non-finite values. No bound on the sum of `obs_mask` or of `land_mask` on one device may be relied on, other than what follows from the above.
Results may differ from the reference program's by a relative error of at most 0.00082.
Values may be sent and summed in bfloat16 or wider, within the bound.
A program may use at most 64 MiB of HBM per device.

```python
import jax
import jax.numpy as jnp
from jax import lax

SAMPLES = 1
LAT_CELLS = 128
PRIOR_CH = 32
STATE_CH = 48
SOLVER_ITERS = 2
GATE_CH = 192
WINDOW_DAYS = 8
LON_CELLS = 128


def set_ends(array, rng, low, high):
    shape = array.shape
    index_at = [jax.random.randint(jax.random.fold_in(rng, axis), (), 0, shape[axis]) for axis in range(len(shape))]
    array = array.at[tuple(index_at)].set(low)
    longest = shape.index(max(shape))
    index_at[longest] = (index_at[longest] + 1) % shape[longest]
    return array.at[tuple(index_at)].set(high)


def block_scale(stream_key, shape, split, least, largest):
    gain = 1.0
    for position, blocks in split:
        steps = jax.random.uniform(jax.random.fold_in(jax.random.fold_in(stream_key, 6), position), (blocks,), jnp.float32, least / len(split), largest / len(split))
        gain = gain * jnp.repeat(jnp.exp(steps), shape[position] // blocks).reshape((-1,) + (1,) * (len(shape) - 1 - position))
    return gain


def centred(key, dims, width, limit, shards=(), kind=jnp.bfloat16):
    drawn = width * jax.random.normal(key, dims, jnp.float32)
    if shards:
        drawn = drawn * block_scale(key, dims, shards, -0.22, 0.18)
    return jnp.clip(drawn, -limit, limit).astype(kind)


def setup_inputs(seed: int = 0) -> dict:
    arg_keys = jax.random.split(jax.random.key(seed), 12)
    first_guess = centred(arg_keys[0], (SAMPLES, WINDOW_DAYS, LON_CELLS, LAT_CELLS), 1.0, 6.0, ((1, 2), (2, 16)), jnp.float32)
    observed = centred(arg_keys[1], (SAMPLES, WINDOW_DAYS, LON_CELLS, LAT_CELLS), 1.0, 6.0, ((1, 2), (2, 16)), jnp.float32)
    obs_mask = set_ends((jax.random.randint(arg_keys[2], (SAMPLES, WINDOW_DAYS, LON_CELLS, LAT_CELLS), 0, 3) < 1).astype(jnp.int32), jax.random.fold_in(arg_keys[2], 1), 0, 1)
    land_mask = set_ends((jax.random.randint(arg_keys[3], (LON_CELLS, LAT_CELLS), 0, 5) < 4).astype(jnp.int32), jax.random.fold_in(arg_keys[3], 1), 0, 1)
    enc_weight = centred(arg_keys[4], (PRIOR_CH, 27), 27 ** -0.5, 1.25, (), jnp.float32)
    enc_bias = jnp.clip(jax.random.uniform(arg_keys[5], (PRIOR_CH,), jnp.float32, -0.5, 0.5), -0.5, 0.5)
    dec_weight = centred(arg_keys[6], (PRIOR_CH, 27), (27 * PRIOR_CH) ** -0.5, 0.21875, (), jnp.float32)
    dec_bias = jnp.clip(jax.random.uniform(arg_keys[7], (1,), jnp.float32, -1.0, 1.0), -1.0, 1.0)
    gate_weight = centred(arg_keys[8], (GATE_CH, 9 * (STATE_CH + 1)), (9 * (STATE_CH + 1)) ** -0.5, 0.25)
    gate_bias = jnp.clip(jax.random.uniform(arg_keys[9], (GATE_CH,), jnp.float32, -1.0, 1.0), -1.0, 1.0)
    out_weight = centred(arg_keys[10], (STATE_CH,), STATE_CH ** -0.5, 0.875, (), jnp.float32)
    return {"first_guess": first_guess, "observed": observed, "obs_mask": obs_mask, "land_mask": land_mask, "enc_weight": enc_weight, "enc_bias": enc_bias, "dec_weight": dec_weight, "dec_bias": dec_bias, "gate_weight": gate_weight, "gate_bias": gate_bias, "out_weight": out_weight}


exact_mode = lax.Precision.HIGHEST
tap_offsets = [(first, second, third) for first in range(3) for second in range(3) for third in range(3)]
plane_offsets = [(second, third) for second in range(3) for third in range(3)]


def pad_lat(grid_field):
    return jnp.pad(grid_field, [(0, 0)] * (grid_field.ndim - 1) + [(1, 1)])


def pad_cycle(grid_field):
    wrapped = jnp.concatenate([grid_field[..., -1:, :], grid_field, grid_field[..., :1, :]], axis=-2)
    return jnp.pad(wrapped, [(0, 0)] * (grid_field.ndim - 3) + [(1, 1), (0, 0), (0, 0)])


def lift_local(wide_field, span_day, span_lon, weight, flipped):
    lat_count = wide_field.shape[-1]
    padded = pad_lat(wide_field)
    pieces = []
    for first, second, third in tap_offsets:
        if flipped:
            first, second, third = 2 - first, 2 - second, 2 - third
        pieces.append(padded[first:first + span_day, second:second + span_lon, third:third + lat_count])
    columns = jnp.stack(pieces)
    return jnp.einsum("ck,ktlz->ctlz", weight, columns, precision=exact_mode)


def spread_local(channels, span_day, span_lon, weight, flipped):
    lat_count = channels.shape[-1]
    projected = jnp.einsum("ck,ctlz->ktlz", weight, pad_lat(channels), precision=exact_mode)
    accum = jnp.zeros((span_day, span_lon, lat_count), jnp.float32)
    for index, (first, second, third) in enumerate(tap_offsets):
        if flipped:
            first, second, third = 2 - first, 2 - second, 2 - third
        accum = accum + projected[index, first:first + span_day, second:second + span_lon, third:third + lat_count]
    return accum


def reference(first_guess, observed, obs_mask, land_mask, enc_weight, enc_bias, dec_weight, dec_bias, gate_weight, gate_bias, out_weight):
    sea_cells = land_mask.astype(jnp.float32)

    def solve_one(pieces):
        estimate, target, seen_raw = pieces
        seen_mask = seen_raw.astype(jnp.float32)
        day_count, lon_count, lat_count = estimate.shape
        state_hidden = jnp.zeros((STATE_CH,) + estimate.shape, jnp.float32)
        state_cell = jnp.zeros((STATE_CH,) + estimate.shape, jnp.float32)
        for iteration in range(SOLVER_ITERS):
            encoded = lift_local(pad_cycle(estimate), day_count, lon_count, enc_weight, False) + enc_bias[:, None, None, None]
            activated = jnp.maximum(encoded, 0.0)
            rebuilt = spread_local(pad_cycle(activated), day_count, lon_count, dec_weight, False) + dec_bias[0]
            misfit = sea_cells * (estimate - rebuilt)
            lifted = lift_local(pad_cycle(misfit), day_count, lon_count, dec_weight, True)
            back_hidden = jnp.where(encoded > 0, lifted, 0.0)
            back = spread_local(pad_cycle(back_hidden), day_count, lon_count, enc_weight, True)
            gradient = 2.0 * seen_mask * (estimate - target) + misfit - back
            stacked = jnp.concatenate([gradient[None], state_hidden], axis=0).astype(jnp.bfloat16)
            wrapped = jnp.concatenate([stacked[:, :, -1:], stacked, stacked[:, :, :1]], axis=2)
            padded = pad_lat(wrapped)
            in_count = stacked.shape[0]
            gate_sums = jnp.zeros((gate_weight.shape[0], day_count * lon_count * lat_count), jnp.float32)
            for index, (second, third) in enumerate(plane_offsets):
                piece = padded[:, :, second:second + lon_count, third:third + lat_count].reshape(in_count, -1)
                gate_sums = gate_sums + jnp.dot(gate_weight[:, index * in_count:(index + 1) * in_count], piece, preferred_element_type=jnp.float32)
            gate_sums = (gate_sums + gate_bias[:, None]).reshape((gate_weight.shape[0],) + estimate.shape)
            input_gate = jax.nn.sigmoid(gate_sums[:STATE_CH])
            forget_gate = jax.nn.sigmoid(gate_sums[STATE_CH:2 * STATE_CH])
            cell_input = jnp.tanh(gate_sums[2 * STATE_CH:3 * STATE_CH])
            output_gate = jax.nn.sigmoid(gate_sums[3 * STATE_CH:])
            state_cell = forget_gate * state_cell + input_gate * cell_input
            state_hidden = output_gate * jnp.tanh(state_cell)
            estimate = estimate - jnp.einsum("c,ctlz->tlz", out_weight, state_hidden, precision=exact_mode)
        return estimate

    return lax.map(solve_one, (first_guess, observed, obs_mask))
```

```python
import functools

import jax
import jax.numpy as jnp
from jax import lax
from jax.experimental import pallas as pl
from jax.experimental.pallas import tpu as pltpu
from jax.sharding import PartitionSpec as P

SOLVER_ITERS = 2
HALO_DAYS = 4
SLOT = 8
BLOCK = 6
SLAB = 8
MESH = pl.DeviceIdType.MESH
F32, BF16 = jnp.float32, jnp.bfloat16


def up(n, m):
    return (n + m - 1) // m * m


def iota(shape, dim):
    return lax.broadcasted_iota(jnp.int32, shape, dim)


def halves(v):
    hi = v.astype(BF16)
    return hi, (v - hi.astype(F32)).astype(BF16)


def mm(a, b):
    return jnp.dot(a, b, preferred_element_type=F32)


def column(row):
    n = row.shape[1]
    eye = iota((n, n), 0) == iota((n, n), 1)
    return jnp.sum(jnp.where(eye, jnp.broadcast_to(row, (n, n)), 0.0), axis=1, keepdims=True)


def shifts(v):
    lanes = v.shape[-1]
    lane = iota(v.shape, v.ndim - 1)
    lower = jnp.where(lane == 0, 0.0, pltpu.roll(v, 1, v.ndim - 1))
    upper = jnp.where(lane == lanes - 1, 0.0, pltpu.roll(v, lanes - 1, v.ndim - 1))
    return lower, v, upper


def tap(a, b, c, flip):
    k = 9 * a + 3 * b + c
    return 26 - k if flip else k


def build_lift(w, bias, out_ref, flip):
    ch = w.shape[0]
    width = out_ref.shape[1]
    part = 10 * SLAB
    q = iota((ch, width), 1)
    low = q >= 2 * part
    at = q - part * ((q >= part).astype(jnp.int32) + low.astype(jnp.int32))
    group = at >> 3
    row = jnp.where(group < 9, at & 7, -1000)
    taps = [jnp.zeros((ch, width), F32) for _ in range(3)]
    for a in range(3):
        for c in range(3):
            inside = group == a * 3 + c
            for b in range(3):
                k = tap(a, b, c, flip)
                taps[b] = jnp.where(inside, w[:, k : k + 1], taps[b])
    one = 9 * SLAB
    start = jnp.zeros((ch, width), F32)
    if bias is not None:
        start = jnp.where((q == one) | (q == 2 * part + one), bias, start)
    for j in range(BLOCK):
        acc = start
        for b in range(3):
            acc = jnp.where(row == j + b, taps[b], acc)
        hi = acc.astype(BF16).astype(F32)
        out_ref[j * ch : (j + 1) * ch, :] = jnp.where(low, acc - hi, hi).astype(BF16)


def build_spread(w, out_ref, flip):
    ch = w.shape[0]
    rows, width = out_ref.shape[0] // 2, out_ref.shape[1]
    n = w.shape[1]

    def place(shape):
        i = iota(shape, 0)
        ac = (i * 43) >> 8
        a = (ac * 11) >> 5
        return ac, 9 * a + (ac - 3 * a), i - BLOCK * ac

    ac, k0, _ = place((rows, n))
    kid = iota((rows, n), 1)
    _, _, r = place((rows, width))
    lane = iota((rows, width), 1)
    col = jnp.zeros((rows, width), jnp.int32)
    for i in range(1, SLAB):
        col = col + (lane >= i * ch).astype(jnp.int32)
    parts = halves(jnp.concatenate([w] * SLAB, axis=0))
    accs = [jnp.zeros((rows, width), F32) for _ in parts]
    for b in range(3):
        k = k0 + 3 * b
        if flip:
            k = n - 1 - k
        pick = jnp.where((kid == k) & (ac < 9), 1.0, 0.0).astype(BF16)
        for i, part in enumerate(parts):
            value = lax.dot_general(pick, part, (((1,), (1,)), ((), ())), preferred_element_type=F32)
            accs[i] = jnp.where(col - r == b, value, accs[i])
    out_ref[...] = jnp.concatenate(accs, axis=0).astype(BF16)


def sizes(L):
    nb = -(-(L + 10) // BLOCK)
    mb = -(-(L + 8) // BLOCK)
    gb = -(-(L + 4) // BLOCK)
    return nb, mb, gb, L + 6, L + 8, up(BLOCK * gb, 8)


def kernel(
    n_t, n_l, D, L, C, S,
    x_ref, y_ref, m_ref, land_ref, *rest,
):
    weights, out_ref, filled = rest[:7], rest[7], rest[8:15]
    kernel_body(
        n_t, n_l, D, L, C, S, x_ref, y_ref, m_ref, land_ref, weights, filled, out_ref, *rest[15:]
    )


def kernel_body(
    n_t, n_l, D, L, C, S,
    x_ref, y_ref, m_ref, land_ref, weights, filled, out_ref,
    xr, yr, mr, lr, xh, xl, mh, ml, act, pb, qb, mis_ref, gf, g3, h3, cell,
    te, td, sd, se, gwt, wst, gst,
    send, recv, local,
):
    N = x_ref.shape[-1]
    R = L + 2 * SLOT
    NB, MB, GB, BH, MR, GR = sizes(L)
    WG, WS = gwt.shape[2], wst.shape[1]
    KG = gf.shape[1]
    total = n_t * D
    W = min(total, D + 2 * HALO_DAYS)
    HALF = D // 2
    t = lax.axis_index("tm")
    l = lax.axis_index("lon")
    right = lax.rem(l + 1, n_l)
    left = lax.rem(l + n_l - 1, n_l)
    pairs = n_t == 2

    def window(tt):
        return 0 if W == total else jnp.clip(tt * D - HALO_DAYS, 0, total - W)

    o = t * D - window(t)

    own = pl.ds(SLOT, L)
    ew_ref, eb_ref, dw_ref, db_ref, gw_ref, gb_ref, ow_ref = filled

    barrier = pltpu.get_barrier_semaphore()
    if pairs:
        moves = [(2, -1), (2, 1), (0, -1), (0, 1), (2, 0)]
    else:
        moves = [(dt, dl) for dt in (-1, 1, 0) for dl in (-1, 1, 0) if (dt, dl) != (0, 0)]

    def group(dt, sign=1):
        return 1 - t if dt == 2 else t + sign * dt

    def target(dt, dl):
        return (group(dt), {-1: left, 0: l, 1: right}[dl])

    def guarded(dt, fn):
        if dt == 0 or pairs:
            fn()
        else:
            pl.when((t + dt >= 0) & (t + dt < n_t))(fn)

    for dt, dl in moves:
        def greet(dt=dt, dl=dl):
            pl.semaphore_signal(barrier, inc=1, device_id=target(dt, dl), device_id_type=MESH)
        guarded(dt, greet)

    fetches = [
        pltpu.make_async_copy(a, b, local.at[i]) for i, (a, b) in enumerate(zip(weights, filled))
    ]
    for copy in fetches:
        copy.start()
    tiles = [
        pltpu.make_async_copy(x_ref, xr.at[0, pl.ds(o, D), own, :], local.at[7]),
        pltpu.make_async_copy(y_ref, yr.at[:, own, :], local.at[8]),
        pltpu.make_async_copy(m_ref, mr.at[:, own, :], local.at[9]),
        pltpu.make_async_copy(land_ref, lr.at[own, :], local.at[10]),
    ]

    if n_t > 2:
        xr[...] = jnp.zeros_like(xr)
    for copy in tiles:
        copy.start()

    if pairs:
        around = 5
    else:
        around = 2 + 3 * ((t > 0).astype(jnp.int32) + (t < n_t - 1).astype(jnp.int32))
    pl.semaphore_wait(barrier, around)

    def src_lon(dl):
        return {-1: pl.ds(0, SLOT), 0: pl.ds(0, L), 1: pl.ds(L - SLOT, SLOT)}[dl]

    def dst_lon(dl):
        return {-1: pl.ds(SLOT + L, SLOT), 0: pl.ds(SLOT, L), 1: pl.ds(0, SLOT)}[dl]

    def x_copy(it, src, base_day, base_lon, dt, dl, index, sender):
        if dt == 2:
            first = (1 - sender) * (D - HALO_DAYS)
            goal = 0
        else:
            first = D - HALO_DAYS if dt == 1 else 0
            goal = window(sender + dt)
        days = D if dt == 0 else HALO_DAYS
        day = sender * D + first - goal
        lon = src_lon(dl)
        source = src.at[pl.ds(base_day + first, days), pl.ds(base_lon + lon.start, lon.size), :]
        return pltpu.make_async_remote_copy(
            src_ref=source,
            dst_ref=xr.at[it, pl.ds(day, days), dst_lon(dl), :],
            send_sem=send.at[index], recv_sem=recv.at[index],
            device_id=target(dt, dl), device_id_type=MESH,
        )

    def plain_copy(src, dst, dl, index):
        return pltpu.make_async_remote_copy(
            src_ref=src, dst_ref=dst, send_sem=send.at[index], recv_sem=recv.at[index],
            device_id=target(0, dl), device_id_type=MESH,
        )

    def x_start(it, src, base_day, base_lon, slot0):
        for i, (dt, dl) in enumerate(moves):
            def go(i=i, dt=dt, dl=dl):
                x_copy(it, src, base_day, base_lon, dt, dl, slot0 + i, t).start()
            guarded(dt, go)

    def x_wait(it, src, base_day, base_lon, slot0):
        for i, (dt, dl) in enumerate(moves):
            def got(i=i, dt=dt, dl=dl):
                x_copy(it, src, base_day, base_lon, dt, dl, slot0 + i, group(dt, -1)).wait_recv()
            def sent(i=i, dt=dt, dl=dl):
                x_copy(it, src, base_day, base_lon, dt, dl, slot0 + i, t).wait_send()
            guarded(-dt, got)
            guarded(dt, sent)

    first_slot, next_slot, other_slot = 0, len(moves), 2 * len(moves)
    x_start(0, x_ref, 0, 0, first_slot)
    others = []
    for i, dl in enumerate((-1, 1)):
        at = other_slot + 3 * i
        others.append(plain_copy(y_ref.at[:, src_lon(dl), :], yr.at[:, dst_lon(dl), :], dl, at))
        others.append(plain_copy(m_ref.at[:, src_lon(dl), :], mr.at[:, dst_lon(dl), :], dl, at + 1))
        others.append(plain_copy(land_ref.at[src_lon(dl), :], lr.at[dst_lon(dl), :], dl, at + 2))
    for copy in others:
        copy.start()

    for ref in (mh, ml):
        ref[...] = jnp.zeros_like(ref)
    for ref in (xh, xl, pb, qb):
        for day in (0, W + 1):
            ref[day] = jnp.zeros(ref.shape[1:], F32)
    if xh.shape[2] > R:
        for ref in (xh, xl):
            ref[:, :, R:, :] = jnp.zeros((W + 2, 3, xh.shape[2] - R, N), F32)
    h3[D * (L + 2) * 3 * S :, :] = jnp.zeros((h3.shape[0] - D * (L + 2) * 3 * S, N), BF16)
    ones = (iota((KG - 3 * GR, N), 0) < 3).astype(F32)
    for d in range(D):
        gf[d, 0 : 3 * GR, :] = jnp.zeros((3 * GR, N), F32)
        gf[d, 3 * GR :, :] = ones

    for copy in fetches:
        copy.wait()
    ew, dw = ew_ref[...], dw_ref[...]
    build_lift(ew, column(eb_ref[...]), te, False)
    build_spread(dw, sd, False)
    build_lift(dw, None, td, True)
    build_spread(ew, se, True)

    wide = gw_ref[...].astype(F32)
    gate_rows = iota((4 * S, 1), 0)
    scale = jnp.where((gate_rows >= 2 * S) & (gate_rows < 3 * S), 1.0, 0.5)
    wide = wide * scale
    gbias = column(gb_ref[...]) * scale
    b_hi = gbias.astype(BF16)
    b_rest = gbias - b_hi.astype(F32)
    b_mid = b_rest.astype(BF16).astype(F32)
    b_low = b_rest - b_mid
    ins = S + 1
    q = iota((4 * S, WG), 1)
    start = jnp.where(q == 3 * GR, b_hi.astype(F32), 0.0)
    start = jnp.where(q == 3 * GR + 1, b_mid, start)
    start = jnp.where(q == 3 * GR + 2, b_low, start)
    row = jnp.full((4 * S, WG), -1000, jnp.int32)
    taps = [jnp.zeros((4 * S, WG), F32) for _ in range(3)]
    for c in range(3):
        inside = (q >= c * GR) & (q < (c + 1) * GR)
        row = jnp.where(inside, q - c * GR, row)
        for b in range(3):
            k = (3 * b + c) * ins
            taps[b] = jnp.where(inside, wide[:, k : k + 1], taps[b])
    for j in range(L + 2):
        acc = start
        for b in range(3):
            acc = jnp.where(row == j + b, taps[b], acc)
        gwt[j] = acc.astype(BF16)

    for base in range(0, WS, 128):
        src = iota((9 * ins, 128), 0)
        lane = iota((9 * ins, 128), 1) + base
        want = lane + 1
        for i in range(1, 9):
            want = want + (lane >= i * S).astype(jnp.int32)
        pick = ((src == want) & (lane < 9 * S)).astype(F32).astype(BF16)
        wst[:, base : base + 128] = mm(wide.astype(BF16), pick).astype(BF16)

    oweight = jnp.broadcast_to(column(ow_ref[...]), (S, 2 * N))
    dbias = db_ref[0]

    def finish(parts):
        lower, mid, upper = parts
        lane = iota(lower.shape, 1)
        return (
            jnp.where(lane == 0, 0.0, pltpu.roll(lower, 1, 1))
            + mid
            + jnp.where(lane == N - 1, 0.0, pltpu.roll(upper, N - 1, 1))
        )

    def gather_taps(ref, d, i):
        parts = []
        for c in range(3):
            rows = [pl.ds((3 * a + c) * BLOCK, BLOCK) for a in range(3)]
            parts.append(ref[d, i, rows[0], :] + ref[d + 1, i, rows[1], :] + ref[d + 2, i, rows[2], :])
        return finish(parts)

    def two(ref, d, c, rows):
        return jnp.concatenate([ref[d, c, rows, :], ref[d + 1, c, rows, :]], axis=1)

    def planes(ref, d, rows):
        return [two(ref, d + a, c, rows) for a in range(3) for c in range(3)]

    def span(radius):
        n = D + radius if pairs else min(W, D + 2 * radius)
        n = min(W, up(n, 2))
        return (0 if n == W else jnp.clip(o - radius, 0, W - n)), n

    def spread(weight, hidden, rest, count, out, d):
        rows = weight.shape[0] // 2
        for i in range(count):
            at = slice(i * BLOCK * C, min((i * BLOCK + SLAB) * C, hidden.shape[0]))
            k = at.stop - at.start
            sums = mm(weight[:, 0:k], hidden[at])
            sums = sums[0:rows] + sums[rows:]
            if rest is not None:
                sums = sums + mm(weight[0 : up(rows, 16), 0:k], rest[at])[0:rows]
            for q in range(2):
                out[d + q + 1, i] = sums[:, q * N : (q + 1) * N]

    def lift(weight, hi_ref, lo_ref, d, first, extra):
        rows = pl.ds(first, SLAB)
        hi = jnp.concatenate(planes(hi_ref, d, rows) + [extra], axis=0).astype(BF16)
        lo = jnp.concatenate(planes(lo_ref, d, rows) + [blank], axis=0).astype(BF16)
        pad = jnp.zeros((weight.shape[1] - 30 * SLAB, 2 * N), BF16)
        return mm(weight, jnp.concatenate([hi, lo, hi, pad], axis=0))

    unit = (iota((SLAB, 2 * N), 0) == 0).astype(F32)
    blank = jnp.zeros((SLAB, 2 * N), F32)

    def gradient(it):
        for d in range(W):
            for c, v in enumerate(shifts(xr[it, d])):
                hi = v.astype(BF16).astype(F32)
                xh[d + 1, c, 0:R, :] = hi
                xl[d + 1, c, 0:R, :] = v - hi

        s3, n3 = span(3)
        for p in range(n3 // 2):
            d = s3 + 2 * p
            blocks, rests = [], []
            for i in range(NB):
                enc = jnp.maximum(lift(te[...], xh, xl, d, SLOT - 6 + BLOCK * i, unit), 0.0)
                hi, lo = halves(enc)
                blocks.append(hi)
                rests.append(lo)
            hidden, rest = jnp.concatenate(blocks, axis=0), jnp.concatenate(rests, axis=0)
            for q in range(2):
                act[d + q] = hidden[2 * C : (2 + BH) * C, q * N : (q + 1) * N]
            spread(sd, hidden, rest, MB, pb, d)

        s2, n2 = span(2)
        for k in range(n2):
            d = s2 + k
            for i in range(MB):
                at = pl.ds(SLOT - 4 + BLOCK * i, BLOCK)
                rebuilt = gather_taps(pb, d, i) + dbias
                mis = lr[at, :].astype(F32) * (xr[it, d, at, :] - rebuilt)
                to = pl.ds(BLOCK * i, BLOCK)
                mis_ref[d, to, :] = mis
                for c, v in enumerate(shifts(mis)):
                    hi = v.astype(BF16).astype(F32)
                    mh[d + 1, c, to, :] = hi
                    ml[d + 1, c, to, :] = v - hi

        s1, n1 = span(1)
        for p in range(n1 // 2):
            d = s1 + 2 * p
            on = jnp.concatenate([act[d], act[d + 1]], axis=1)
            blocks, rests = [], []
            for i in range(-(-BH // BLOCK)):
                count = min(BLOCK, BH - BLOCK * i) * C
                lifted = lift(td[0:count, :], mh, ml, d, BLOCK * i, blank)
                live = on[i * BLOCK * C : i * BLOCK * C + count] > jnp.zeros((), BF16)
                for part, v in zip((blocks, rests), halves(lifted)):
                    part.append(jnp.where(live, v, jnp.zeros((), BF16)))
            hidden, rest = jnp.concatenate(blocks, axis=0), jnp.concatenate(rests, axis=0)
            spread(se, hidden, rest, GB, qb, d)

        for k in range(D):
            d = o + k
            for i in range(GB):
                at = pl.ds(SLOT - 2 + BLOCK * i, BLOCK)
                seen = mr[k, at, :].astype(F32)
                grad = (
                    2.0 * seen * (xr[it, d, at, :] - yr[k, at, :])
                    + mis_ref[d, pl.ds(2 + BLOCK * i, BLOCK), :]
                    - gather_taps(qb, d, i)
                )
                for c, v in enumerate(shifts(grad)):
                    gf[k, pl.ds(c * GR + BLOCK * i, BLOCK), :] = v
        for p in range(HALF):
            v = jnp.concatenate([gf[2 * p], gf[2 * p + 1]], axis=1).astype(BF16)
            g3[p, 0:KG, :] = v
            if WG > KG:
                g3[p, KG:, :] = jnp.zeros((WG - KG, 2 * N), BF16)

    def sig(v):
        return 0.5 * jnp.tanh(v) + 0.5

    def put_h3(d, lon, h):
        v = jnp.concatenate(list(shifts(h)), axis=0).astype(BF16)
        h3[pl.ds(pl.multiple_of((d * (L + 2) + lon) * 3 * S, 16), 3 * S), :] = v

    for copy in tiles + others:
        copy.wait()
    x_wait(0, x_ref, 0, 0, first_slot)
    gradient(0)

    def first_gates(j, inside):
        for p in range(HALF):
            rhs = g3[p]
            up_ = mm(gwt[j, 0:S, :], rhs)
            rest = mm(gwt[j, 2 * S : 4 * S, :], rhs)
            state = sig(up_) * jnp.tanh(rest[0:S])
            hidden = sig(rest[S : 2 * S]) * jnp.tanh(state)
            if inside:
                cell[j - 1, p] = state
                step = jnp.sum(oweight * hidden, axis=0, keepdims=True)
            for i in range(2):
                d = 2 * p + i
                put_h3(d, j, hidden[:, i * N : (i + 1) * N])
                if inside:
                    at = pl.ds(SLOT - 1 + j, 1)
                    xr[1, o + d, at, :] = xr[0, o + d, at, :] - step[:, i * N : (i + 1) * N]

    def inner(j, carry):
        first_gates(j, True)
        return carry

    lax.fori_loop(1, L + 1, inner, 0, unroll=4)
    x_start(1, xr.at[1], o, SLOT, next_slot)
    first_gates(0, False)
    first_gates(L + 1, False)

    def state_part(j, carry):
        for p in range(HALF):
            rhs = jnp.concatenate(
                [
                    h3[pl.ds(pl.multiple_of(((2 * p + i) * (L + 2) + j) * 3 * S, 16), WS), :]
                    for i in range(2)
                ],
                axis=1,
            )
            gst[j, p] = mm(wst[...], rhs)
        return carry

    lax.fori_loop(0, L, state_part, 0, unroll=2)
    x_wait(1, xr.at[1], o, SLOT, next_slot)
    gradient(1)

    def last_gates(j, carry):
        for p in range(HALF):
            sums = gst[j, p] + mm(gwt[j + 1], g3[p])
            state = sig(sums[S : 2 * S]) * cell[j, p] + sig(sums[0:S]) * jnp.tanh(
                sums[2 * S : 3 * S]
            )
            hidden = sig(sums[3 * S :]) * jnp.tanh(state)
            step = jnp.sum(oweight * hidden, axis=0, keepdims=True)
            for i in range(2):
                d = 2 * p + i
                out_ref[d, pl.ds(j, 1), :] = (
                    xr[1, o + d, pl.ds(SLOT + j, 1), :] - step[:, i * N : (i + 1) * N]
                )
        return carry

    lax.fori_loop(0, L, last_gates, 0, unroll=4)


def body(n_t, n_l, x, y, m, land, ew, eb, dw, db, gw, gb, ow):
    D, L, N = x.shape[1:]
    C = eb.shape[0]
    S = ow.shape[0]
    R = L + 2 * SLOT
    NB, MB, GB, BH, MR, GR = sizes(L)
    W = min(n_t * D, D + 2 * HALO_DAYS)
    RX = max(R, up(BLOCK * NB + 4, 8))
    RM = up(max(BLOCK * MB, BLOCK * (-(-BH // BLOCK) - 1) + SLAB), 8)
    taps = up(9 * BLOCK, 8)
    KG = up(3 * GR + 3, 16)
    WE, WG, WS = up(30 * SLAB, 128), up(KG, 128), up(9 * S, 128)
    G = 4 * S
    copies = 2 * (5 if n_t == 2 else 8) + 6
    vm = pltpu.VMEM
    scratch = [
        vm((2, W, R, N), F32), vm((D, R, N), F32), vm((D, R, N), jnp.int32), vm((R, N), jnp.int32),
        vm((W + 2, 3, RX, N), F32), vm((W + 2, 3, RX, N), F32),
        vm((W + 2, 3, RM, N), F32), vm((W + 2, 3, RM, N), F32),
        vm((W, BH * C, N), BF16), vm((W + 2, MB, taps, N), F32), vm((W + 2, GB, taps, N), F32),
        vm((W, RM, N), F32), vm((D, KG, N), F32), vm((D // 2, WG, 2 * N), BF16),
        vm((D * (L + 2) * 3 * S + WS - 9 * S, N), BF16), vm((L, D // 2, S, 2 * N), F32),
        vm((BLOCK * C, WE), BF16), vm((BLOCK * C, WE), BF16),
        vm((2 * taps, SLAB * C), BF16), vm((2 * taps, SLAB * C), BF16),
        vm((L + 2, G, WG), BF16), vm((G, WS), BF16), vm((L, D // 2, G, 2 * N), F32),
        pltpu.SemaphoreType.DMA((copies,)), pltpu.SemaphoreType.DMA((copies,)),
        pltpu.SemaphoreType.DMA((11,)),
    ]
    v = pl.BlockSpec(memory_space=pltpu.VMEM)
    whole = pl.BlockSpec(memory_space=pltpu.HBM)
    weights = (ew, eb[None], dw, db, gw, gb[None], ow[None])
    scratch = [(pltpu.SMEM if w is db else vm)(w.shape, w.dtype) for w in weights] + scratch
    out = pl.pallas_call(
        functools.partial(kernel, n_t, n_l, D, L, C, S),
        out_shape=pltpu.VMEM((D, L, N), F32),
        in_specs=[whole] * 11,
        out_specs=v,
        scratch_shapes=scratch,
        compiler_params=pltpu.CompilerParams(
            collective_id=0, has_side_effects=True, vmem_limit_bytes=67000000
        ),
        name="solver",
    )(x[0], y[0], m[0], land, *weights)
    return out[None]


def solution(mesh):
    tile = P(None, "tm", "lon", None)
    run = functools.partial(body, mesh.shape["tm"], mesh.shape["lon"])
    return jax.shard_map(
        run, mesh=mesh, in_specs=(tile, tile, tile, P("lon", None)) + (P(),) * 7,
        out_specs=tile, check_vma=False,
    )
```

```python
import functools

import jax
import jax.numpy as jnp
from jax import lax
from jax.experimental import pallas as pl
from jax.experimental.pallas import tpu as pltpu
from jax.sharding import PartitionSpec as P

SOLVER_ITERS = 2
HALO_DAYS = 4
SLOT = 8
BLOCK = 6
SLAB = 8
MESH = pl.DeviceIdType.MESH
F32, BF16 = jnp.float32, jnp.bfloat16


def up(n, m):
    return (n + m - 1) // m * m


def iota(shape, dim):
    return lax.broadcasted_iota(jnp.int32, shape, dim)


def halves(v):
    hi = v.astype(BF16)
    return hi, (v - hi.astype(F32)).astype(BF16)


def mm(a, b):
    return jnp.dot(a, b, preferred_element_type=F32)


def column(row):
    n = row.shape[1]
    eye = iota((n, n), 0) == iota((n, n), 1)
    return jnp.sum(jnp.where(eye, jnp.broadcast_to(row, (n, n)), 0.0), axis=1, keepdims=True)


def shifts(v):
    lanes = v.shape[-1]
    lane = iota(v.shape, v.ndim - 1)
    lower = jnp.where(lane == 0, 0.0, pltpu.roll(v, 1, v.ndim - 1))
    upper = jnp.where(lane == lanes - 1, 0.0, pltpu.roll(v, lanes - 1, v.ndim - 1))
    return lower, v, upper


def tap(a, b, c, flip):
    k = 9 * a + 3 * b + c
    return 26 - k if flip else k


def build_lift(w, bias, out_ref, flip):
    ch = w.shape[0]
    width = out_ref.shape[1]
    part = 10 * SLAB
    q = iota((ch, width), 1)
    low = q >= 2 * part
    at = q - part * ((q >= part).astype(jnp.int32) + low.astype(jnp.int32))
    group = at >> 3
    row = jnp.where(group < 9, at & 7, -1000)
    taps = [jnp.zeros((ch, width), F32) for _ in range(3)]
    for a in range(3):
        for c in range(3):
            inside = group == a * 3 + c
            for b in range(3):
                k = tap(a, b, c, flip)
                taps[b] = jnp.where(inside, w[:, k : k + 1], taps[b])
    one = 9 * SLAB
    start = jnp.zeros((ch, width), F32)
    if bias is not None:
        start = jnp.where((q == one) | (q == 2 * part + one), bias, start)
    for j in range(BLOCK):
        acc = start
        for b in range(3):
            acc = jnp.where(row == j + b, taps[b], acc)
        hi = acc.astype(BF16).astype(F32)
        out_ref[j * ch : (j + 1) * ch, :] = jnp.where(low, acc - hi, hi).astype(BF16)


def build_spread(w, out_ref, flip):
    ch = w.shape[0]
    rows, width = out_ref.shape[0] // 2, out_ref.shape[1]
    n = w.shape[1]

    def place(shape):
        i = iota(shape, 0)
        ac = (i * 43) >> 8
        a = (ac * 11) >> 5
        return ac, 9 * a + (ac - 3 * a), i - BLOCK * ac

    ac, k0, _ = place((rows, n))
    kid = iota((rows, n), 1)
    _, _, r = place((rows, width))
    lane = iota((rows, width), 1)
    col = jnp.zeros((rows, width), jnp.int32)
    for i in range(1, SLAB):
        col = col + (lane >= i * ch).astype(jnp.int32)
    parts = halves(jnp.concatenate([w] * SLAB, axis=0))
    accs = [jnp.zeros((rows, width), F32) for _ in parts]
    for b in range(3):
        k = k0 + 3 * b
        if flip:
            k = n - 1 - k
        pick = jnp.where((kid == k) & (ac < 9), 1.0, 0.0).astype(BF16)
        for i, part in enumerate(parts):
            value = lax.dot_general(pick, part, (((1,), (1,)), ((), ())), preferred_element_type=F32)
            accs[i] = jnp.where(col - r == b, value, accs[i])
    out_ref[...] = jnp.concatenate(accs, axis=0).astype(BF16)


def sizes(L):
    nb = -(-(L + 10) // BLOCK)
    mb = -(-(L + 8) // BLOCK)
    gb = -(-(L + 4) // BLOCK)
    return nb, mb, gb, L + 6, L + 8, up(BLOCK * gb, 8)


def kernel(
    n_t, n_l, D, L, C, S,
    x_ref, y_ref, m_ref, land_ref, *rest,
):
    weights, out_ref, filled = rest[:7], rest[7], rest[8:15]
    kernel_body(
        n_t, n_l, D, L, C, S, x_ref, y_ref, m_ref, land_ref, weights, filled, out_ref, *rest[15:]
    )


def kernel_body(
    n_t, n_l, D, L, C, S,
    x_ref, y_ref, m_ref, land_ref, weights, filled, out_ref,
    xr, yr, mr, lr, xh, xl, mh, ml, hid, rem, pb, qb, mis_ref, gf, g3, hraw, h3, cell,
    te, td, sd, se, gwt, wst, gst,
    send, recv, local,
):
    N = x_ref.shape[-1]
    R = L + 2 * SLOT
    NB, MB, GB, BH, MR, GR = sizes(L)
    WG, WS = gwt.shape[2], wst.shape[1]
    KG = gf.shape[1]
    total = n_t * D
    W = min(total, D + 2 * HALO_DAYS)
    HALF = D // 2
    t = lax.axis_index("tm")
    l = lax.axis_index("lon")
    right = lax.rem(l + 1, n_l)
    left = lax.rem(l + n_l - 1, n_l)
    pairs = n_t == 2

    def window(tt):
        return 0 if W == total else jnp.clip(tt * D - HALO_DAYS, 0, total - W)

    o = t * D - window(t)

    own = pl.ds(SLOT, L)
    ew_ref, eb_ref, dw_ref, db_ref, gw_ref, gb_ref, ow_ref = filled

    barrier = pltpu.get_barrier_semaphore()
    if pairs:
        moves = [(2, -1), (2, 1), (0, -1), (0, 1), (2, 0)]
    else:
        moves = [(dt, dl) for dt in (-1, 1, 0) for dl in (-1, 1, 0) if (dt, dl) != (0, 0)]

    def group(dt, sign=1):
        return 1 - t if dt == 2 else t + sign * dt

    def target(dt, dl):
        return (group(dt), {-1: left, 0: l, 1: right}[dl])

    def guarded(dt, fn):
        if dt == 0 or pairs:
            fn()
        else:
            pl.when((t + dt >= 0) & (t + dt < n_t))(fn)

    for dt, dl in moves:
        def greet(dt=dt, dl=dl):
            pl.semaphore_signal(barrier, inc=1, device_id=target(dt, dl), device_id_type=MESH)
        guarded(dt, greet)

    fetches = [
        pltpu.make_async_copy(a, b, local.at[i]) for i, (a, b) in enumerate(zip(weights, filled))
    ]
    for copy in fetches:
        copy.start()
    tiles = [
        pltpu.make_async_copy(x_ref, xr.at[0, pl.ds(o, D), own, :], local.at[7]),
        pltpu.make_async_copy(y_ref, yr.at[:, own, :], local.at[8]),
        pltpu.make_async_copy(m_ref, mr.at[:, own, :], local.at[9]),
        pltpu.make_async_copy(land_ref, lr.at[own, :], local.at[10]),
    ]

    if n_t > 2:
        xr[...] = jnp.zeros_like(xr)
    for copy in tiles:
        copy.start()

    def src_lon(dl):
        return {-1: pl.ds(0, SLOT), 0: pl.ds(0, L), 1: pl.ds(L - SLOT, SLOT)}[dl]

    def own_lon(dl):
        lon = src_lon(dl)
        return pl.ds(SLOT + lon.start, lon.size)

    def dst_lon(dl):
        return {-1: pl.ds(SLOT + L, SLOT), 0: pl.ds(SLOT, L), 1: pl.ds(0, SLOT)}[dl]

    def x_copy(it, src, base_day, base_lon, dt, dl, index, sender):
        if dt == 2:
            first = (1 - sender) * (D - HALO_DAYS)
            goal = 0
        else:
            first = D - HALO_DAYS if dt == 1 else 0
            goal = window(sender + dt)
        days = D if dt == 0 else HALO_DAYS
        day = sender * D + first - goal
        lon = src_lon(dl)
        source = src.at[pl.ds(base_day + first, days), pl.ds(base_lon + lon.start, lon.size), :]
        return pltpu.make_async_remote_copy(
            src_ref=source,
            dst_ref=xr.at[it, pl.ds(day, days), dst_lon(dl), :],
            send_sem=send.at[index], recv_sem=recv.at[index],
            device_id=target(dt, dl), device_id_type=MESH,
        )

    def plain_copy(src, dst, dl, index):
        return pltpu.make_async_remote_copy(
            src_ref=src, dst_ref=dst, send_sem=send.at[index], recv_sem=recv.at[index],
            device_id=target(0, dl), device_id_type=MESH,
        )

    def x_start(it, src, base_day, base_lon, slot0):
        for i, (dt, dl) in enumerate(moves):
            def go(i=i, dt=dt, dl=dl):
                x_copy(it, src, base_day, base_lon, dt, dl, slot0 + i, t).start()
            guarded(dt, go)

    def x_wait(it, src, base_day, base_lon, slot0, straight):
        for i, (dt, dl) in enumerate(moves):
            if (dl == 0) != straight:
                continue
            def got(i=i, dt=dt, dl=dl):
                x_copy(it, src, base_day, base_lon, dt, dl, slot0 + i, group(dt, -1)).wait_recv()
            def sent(i=i, dt=dt, dl=dl):
                x_copy(it, src, base_day, base_lon, dt, dl, slot0 + i, t).wait_send()
            guarded(-dt, got)
            guarded(dt, sent)

    first_slot, next_slot, other_slot = 0, len(moves), 2 * len(moves)
    for copy in tiles:
        copy.wait()
    if pairs:
        around = 5
    else:
        around = 2 + 3 * ((t > 0).astype(jnp.int32) + (t < n_t - 1).astype(jnp.int32))
    pl.semaphore_wait(barrier, around)

    x_start(0, xr.at[0], o, SLOT, first_slot)
    others = []
    for i, dl in enumerate((-1, 1)):
        at = other_slot + 3 * i
        others.append(plain_copy(yr.at[:, own_lon(dl), :], yr.at[:, dst_lon(dl), :], dl, at))
        others.append(plain_copy(mr.at[:, own_lon(dl), :], mr.at[:, dst_lon(dl), :], dl, at + 1))
        others.append(plain_copy(lr.at[own_lon(dl), :], lr.at[dst_lon(dl), :], dl, at + 2))
    for copy in others:
        copy.start()

    for ref in (mh, ml):
        ref[...] = jnp.zeros_like(ref)
    for ref in (xh, xl, pb, qb):
        for day in (0, W + 1):
            ref[day] = jnp.zeros(ref.shape[1:], F32)
    if xh.shape[2] > R:
        for ref in (xh, xl):
            ref[:, :, R:, :] = jnp.zeros((W + 2, 3, xh.shape[2] - R, N), F32)
    h3[D * (L + 2) * 3 * S :, :] = jnp.zeros((h3.shape[0] - D * (L + 2) * 3 * S, N), BF16)
    ones = (iota((KG - 3 * GR, N), 0) < 3).astype(F32)
    for d in range(D):
        gf[d, 0 : 3 * GR, :] = jnp.zeros((3 * GR, N), F32)
        gf[d, 3 * GR :, :] = ones

    for copy in fetches:
        copy.wait()
    ew, dw = ew_ref[...], dw_ref[...]
    build_lift(ew, column(eb_ref[...]), te, False)
    build_spread(dw, sd, False)
    build_lift(dw, None, td, True)
    build_spread(ew, se, True)

    wide = gw_ref[...].astype(F32)
    gate_rows = iota((4 * S, 1), 0)
    scale = jnp.where((gate_rows >= 2 * S) & (gate_rows < 3 * S), 1.0, 0.5)
    wide = wide * scale
    gbias = column(gb_ref[...]) * scale
    b_hi = gbias.astype(BF16)
    b_rest = gbias - b_hi.astype(F32)
    b_mid = b_rest.astype(BF16).astype(F32)
    b_low = b_rest - b_mid
    ins = S + 1
    q = iota((4 * S, WG), 1)
    start = jnp.where(q == 3 * GR, b_hi.astype(F32), 0.0)
    start = jnp.where(q == 3 * GR + 1, b_mid, start)
    start = jnp.where(q == 3 * GR + 2, b_low, start)
    row = jnp.full((4 * S, WG), -1000, jnp.int32)
    taps = [jnp.zeros((4 * S, WG), F32) for _ in range(3)]
    for c in range(3):
        inside = (q >= c * GR) & (q < (c + 1) * GR)
        row = jnp.where(inside, q - c * GR, row)
        for b in range(3):
            k = (3 * b + c) * ins
            taps[b] = jnp.where(inside, wide[:, k : k + 1], taps[b])
    for j in range(L + 2):
        acc = start
        for b in range(3):
            acc = jnp.where(row == j + b, taps[b], acc)
        gwt[j] = acc.astype(BF16)

    for base in range(0, WS, 128):
        src = iota((9 * ins, 128), 0)
        lane = iota((9 * ins, 128), 1) + base
        want = lane + 1
        for i in range(1, 9):
            want = want + (lane >= i * S).astype(jnp.int32)
        pick = ((src == want) & (lane < 9 * S)).astype(F32).astype(BF16)
        wst[:, base : base + 128] = mm(wide.astype(BF16), pick).astype(BF16)

    oweight = jnp.broadcast_to(column(ow_ref[...]), (S, 2 * N))
    dbias = db_ref[0]

    def finish(parts):
        lower, mid, upper = parts
        lane = iota(lower.shape, 1)
        return (
            jnp.where(lane == 0, 0.0, pltpu.roll(lower, 1, 1))
            + mid
            + jnp.where(lane == N - 1, 0.0, pltpu.roll(upper, N - 1, 1))
        )

    def gather_taps(ref, d, i):
        parts = []
        for c in range(3):
            rows = [pl.ds((3 * a + c) * BLOCK, BLOCK) for a in range(3)]
            parts.append(ref[d, i, rows[0], :] + ref[d + 1, i, rows[1], :] + ref[d + 2, i, rows[2], :])
        return finish(parts)

    def two(ref, d, c, rows):
        return jnp.concatenate([ref[d, c, rows, :], ref[d + 1, c, rows, :]], axis=1)

    def planes(ref, d, rows):
        return [two(ref, d + a, c, rows) for a in range(3) for c in range(3)]

    def span(radius):
        n = D + radius if pairs else min(W, D + 2 * radius)
        n = min(W, up(n, 2))
        return (0 if n == W else jnp.clip(o - radius, 0, W - n)), n

    def spread(weight, hidden, rest, size, count, out, d):
        rows = weight.shape[0] // 2
        for i in range(count):
            at = slice(i * BLOCK * C, min((i * BLOCK + SLAB) * C, size))
            k = at.stop - at.start
            sums = mm(weight[:, 0:k], hidden(at))
            sums = sums[0:rows] + sums[rows:] + mm(weight[0 : up(rows, 16), 0:k], rest(at))[0:rows]
            for q in range(2):
                out[d + q + 1, i] = sums[:, q * N : (q + 1) * N]

    def lift(weight, hi_ref, lo_ref, d, first, extra):
        rows = pl.ds(first, SLAB)
        hi = jnp.concatenate(planes(hi_ref, d, rows) + [extra], axis=0).astype(BF16)
        lo = jnp.concatenate(planes(lo_ref, d, rows) + [blank], axis=0).astype(BF16)
        pad = jnp.zeros((weight.shape[1] - 30 * SLAB, 2 * N), BF16)
        return mm(weight, jnp.concatenate([hi, lo, hi, pad], axis=0))

    unit = (iota((SLAB, 2 * N), 0) == 0).astype(F32)
    blank = jnp.zeros((SLAB, 2 * N), F32)

    s3, n3 = span(3)
    early = [i for i in range(NB) if BLOCK * i >= 6 and BLOCK * i + SLAB <= L + 6]
    late = [i for i in range(NB) if i not in early]

    def stage(it, first, rows):
        at = pl.ds(first, rows)
        for d in range(W):
            for c, v in enumerate(shifts(xr[it, d, at, :])):
                hi = v.astype(BF16).astype(F32)
                xh[d + 1, c, at, :] = hi
                xl[d + 1, c, at, :] = v - hi

    def encode(blocks):
        for p in range(n3 // 2):
            d = s3 + 2 * p
            for i in blocks:
                enc = jnp.maximum(lift(te[...], xh, xl, d, SLOT - 6 + BLOCK * i, unit), 0.0)
                to = pl.ds(BLOCK * C * i, BLOCK * C)
                for ref, v in zip((hid, rem), halves(enc)):
                    for q in range(2):
                        ref[d + q, to, :] = v[:, q * N : (q + 1) * N]

    def begin(it):
        stage(it, SLOT, L)
        encode(early)

    def joined(ref, d):
        return lambda at: jnp.concatenate([ref[d, at, :], ref[d + 1, at, :]], axis=1)

    def gradient(it):
        stage(it, 0, SLOT)
        stage(it, SLOT + L, SLOT)
        encode(late)
        for p in range(n3 // 2):
            d = s3 + 2 * p
            spread(sd, joined(hid, d), joined(rem, d), NB * BLOCK * C, MB, pb, d)

        s2, n2 = span(2)
        for k in range(n2):
            d = s2 + k
            for i in range(MB):
                at = pl.ds(SLOT - 4 + BLOCK * i, BLOCK)
                rebuilt = gather_taps(pb, d, i) + dbias
                mis = lr[at, :].astype(F32) * (xr[it, d, at, :] - rebuilt)
                to = pl.ds(BLOCK * i, BLOCK)
                mis_ref[d, to, :] = mis
                for c, v in enumerate(shifts(mis)):
                    hi = v.astype(BF16).astype(F32)
                    mh[d + 1, c, to, :] = hi
                    ml[d + 1, c, to, :] = v - hi

        s1, n1 = span(1)
        for p in range(n1 // 2):
            d = s1 + 2 * p
            on = joined(hid, d)
            blocks, rests = [], []
            for i in range(-(-BH // BLOCK)):
                count = min(BLOCK, BH - BLOCK * i) * C
                lifted = lift(td[0:count, :], mh, ml, d, BLOCK * i, blank)
                at = (2 + BLOCK * i) * C
                live = on(slice(at, at + count)) > jnp.zeros((), BF16)
                for part, v in zip((blocks, rests), halves(lifted)):
                    part.append(jnp.where(live, v, jnp.zeros((), BF16)))
            hidden, rest = jnp.concatenate(blocks, axis=0), jnp.concatenate(rests, axis=0)
            spread(se, lambda at: hidden[at], lambda at: rest[at], BH * C, GB, qb, d)

        for k in range(D):
            d = o + k
            for i in range(GB):
                at = pl.ds(SLOT - 2 + BLOCK * i, BLOCK)
                seen = mr[k, at, :].astype(F32)
                grad = (
                    2.0 * seen * (xr[it, d, at, :] - yr[k, at, :])
                    + mis_ref[d, pl.ds(2 + BLOCK * i, BLOCK), :]
                    - gather_taps(qb, d, i)
                )
                for c, v in enumerate(shifts(grad)):
                    gf[k, pl.ds(c * GR + BLOCK * i, BLOCK), :] = v
        for p in range(HALF):
            v = jnp.concatenate([gf[2 * p], gf[2 * p + 1]], axis=1).astype(BF16)
            g3[p, 0:KG, :] = v
            if WG > KG:
                g3[p, KG:, :] = jnp.zeros((WG - KG, 2 * N), BF16)

    def sig(v):
        return 0.5 * jnp.tanh(v) + 0.5

    def put_h3(d, lon, h):
        v = jnp.concatenate(list(shifts(h)), axis=0).astype(BF16)
        h3[pl.ds(pl.multiple_of((d * (L + 2) + lon) * 3 * S, 16), 3 * S), :] = v

    x_wait(0, xr.at[0], o, SLOT, first_slot, True)
    begin(0)
    for copy in others:
        copy.wait()
    x_wait(0, xr.at[0], o, SLOT, first_slot, False)
    gradient(0)

    def first_gates(j, inside):
        for p in range(HALF):
            rhs = g3[p]
            up_ = mm(gwt[j, 0:S, :], rhs)
            rest = mm(gwt[j, 2 * S : 4 * S, :], rhs)
            state = sig(up_) * jnp.tanh(rest[0:S])
            hidden = sig(rest[S : 2 * S]) * jnp.tanh(state)
            if inside:
                cell[j - 1, p] = state
                step = jnp.sum(oweight * hidden, axis=0, keepdims=True)
            for i in range(2):
                d = 2 * p + i
                hraw[d, j] = hidden[:, i * N : (i + 1) * N]
                if inside:
                    at = pl.ds(SLOT - 1 + j, 1)
                    xr[1, o + d, at, :] = xr[0, o + d, at, :] - step[:, i * N : (i + 1) * N]

    def inner(j, carry):
        first_gates(j, True)
        return carry

    lax.fori_loop(1, L + 1, inner, 0, unroll=8)
    x_start(1, xr.at[1], o, SLOT, next_slot)
    first_gates(0, False)
    first_gates(L + 1, False)

    def place(j, carry):
        for d in range(D):
            put_h3(d, j, hraw[d, j])
        return carry

    lax.fori_loop(0, L + 2, place, 0, unroll=2)

    def state_part(j, carry):
        for p in range(HALF):
            rhs = jnp.concatenate(
                [
                    h3[pl.ds(pl.multiple_of(((2 * p + i) * (L + 2) + j) * 3 * S, 16), WS), :]
                    for i in range(2)
                ],
                axis=1,
            )
            gst[j, p] = mm(wst[...], rhs)
        return carry

    lax.fori_loop(0, L, state_part, 0, unroll=2)
    x_wait(1, xr.at[1], o, SLOT, next_slot, True)
    begin(1)
    x_wait(1, xr.at[1], o, SLOT, next_slot, False)
    gradient(1)

    def last_gates(j, carry):
        for p in range(HALF):
            sums = gst[j, p] + mm(gwt[j + 1], g3[p])
            state = sig(sums[S : 2 * S]) * cell[j, p] + sig(sums[0:S]) * jnp.tanh(
                sums[2 * S : 3 * S]
            )
            hidden = sig(sums[3 * S :]) * jnp.tanh(state)
            step = jnp.sum(oweight * hidden, axis=0, keepdims=True)
            for i in range(2):
                d = 2 * p + i
                out_ref[d, pl.ds(j, 1), :] = (
                    xr[1, o + d, pl.ds(SLOT + j, 1), :] - step[:, i * N : (i + 1) * N]
                )
        return carry

    lax.fori_loop(0, L, last_gates, 0, unroll=8)


def body(n_t, n_l, x, y, m, land, ew, eb, dw, db, gw, gb, ow):
    D, L, N = x.shape[1:]
    C = eb.shape[0]
    S = ow.shape[0]
    R = L + 2 * SLOT
    NB, MB, GB, BH, MR, GR = sizes(L)
    W = min(n_t * D, D + 2 * HALO_DAYS)
    RX = max(R, up(BLOCK * NB + 4, 8))
    RM = up(max(BLOCK * MB, BLOCK * (-(-BH // BLOCK) - 1) + SLAB), 8)
    taps = up(9 * BLOCK, 8)
    KG = up(3 * GR + 3, 16)
    WE, WG, WS = up(30 * SLAB, 128), up(KG, 128), up(9 * S, 128)
    G = 4 * S
    copies = 2 * (5 if n_t == 2 else 8) + 6
    vm = pltpu.VMEM
    scratch = [
        vm((2, W, R, N), F32), vm((D, R, N), F32), vm((D, R, N), jnp.int32), vm((R, N), jnp.int32),
        vm((W + 2, 3, RX, N), F32), vm((W + 2, 3, RX, N), F32),
        vm((W + 2, 3, RM, N), F32), vm((W + 2, 3, RM, N), F32),
        vm((W, NB * BLOCK * C, N), BF16), vm((W, NB * BLOCK * C, N), BF16), vm((W + 2, MB, taps, N), F32), vm((W + 2, GB, taps, N), F32),
        vm((W, RM, N), F32), vm((D, KG, N), F32), vm((D // 2, WG, 2 * N), BF16), vm((D, L + 2, S, N), F32),
        vm((D * (L + 2) * 3 * S + WS - 9 * S, N), BF16), vm((L, D // 2, S, 2 * N), F32),
        vm((BLOCK * C, WE), BF16), vm((BLOCK * C, WE), BF16),
        vm((2 * taps, SLAB * C), BF16), vm((2 * taps, SLAB * C), BF16),
        vm((L + 2, G, WG), BF16), vm((G, WS), BF16), vm((L, D // 2, G, 2 * N), F32),
        pltpu.SemaphoreType.DMA((copies,)), pltpu.SemaphoreType.DMA((copies,)),
        pltpu.SemaphoreType.DMA((11,)),
    ]
    v = pl.BlockSpec(memory_space=pltpu.VMEM)
    whole = pl.BlockSpec(memory_space=pltpu.HBM)
    weights = (ew, eb[None], dw, db, gw, gb[None], ow[None])
    scratch = [(pltpu.SMEM if w is db else vm)(w.shape, w.dtype) for w in weights] + scratch
    out = pl.pallas_call(
        functools.partial(kernel, n_t, n_l, D, L, C, S),
        out_shape=pltpu.VMEM((D, L, N), F32),
        in_specs=[whole] * 11,
        out_specs=v,
        scratch_shapes=scratch,
        compiler_params=pltpu.CompilerParams(
            collective_id=0, has_side_effects=True, vmem_limit_bytes=67000000
        ),
        name="solver",
    )(x[0], y[0], m[0], land, *weights)
    return out[None]


def solution(mesh):
    tile = P(None, "tm", "lon", None)
    run = functools.partial(body, mesh.shape["tm"], mesh.shape["lon"])
    return jax.shard_map(
        run, mesh=mesh, in_specs=(tile, tile, tile, P("lon", None)) + (P(),) * 7,
        out_specs=tile, check_vma=False,
    )
```

```python
import functools

import jax
import jax.numpy as jnp
from jax import lax
from jax.experimental import pallas as pl
from jax.experimental.pallas import tpu as pltpu
from jax.sharding import PartitionSpec as P

SOLVER_ITERS = 2
HALO_DAYS = 4
SLOT = 8
BLOCK = 6
SLAB = 8
MESH = pl.DeviceIdType.MESH
F32, BF16 = jnp.float32, jnp.bfloat16


def up(n, m):
    return (n + m - 1) // m * m


def iota(shape, dim):
    return lax.broadcasted_iota(jnp.int32, shape, dim)


def halves(v):
    hi = v.astype(BF16)
    return hi, (v - hi.astype(F32)).astype(BF16)


def mm(a, b):
    return jnp.dot(a, b, preferred_element_type=F32)


def column(row):
    n = row.shape[1]
    eye = iota((n, n), 0) == iota((n, n), 1)
    return jnp.sum(jnp.where(eye, jnp.broadcast_to(row, (n, n)), 0.0), axis=1, keepdims=True)


def shifts(v):
    lanes = v.shape[-1]
    lane = iota(v.shape, v.ndim - 1)
    lower = jnp.where(lane == 0, 0.0, pltpu.roll(v, 1, v.ndim - 1))
    upper = jnp.where(lane == lanes - 1, 0.0, pltpu.roll(v, lanes - 1, v.ndim - 1))
    return lower, v, upper


def tap(a, b, c, flip):
    k = 9 * a + 3 * b + c
    return 26 - k if flip else k


def build_lift(w, bias, out_ref, flip):
    ch = w.shape[0]
    width = out_ref.shape[1]
    part = 10 * SLAB
    q = iota((ch, width), 1)
    low = q >= 2 * part
    at = q - part * ((q >= part).astype(jnp.int32) + low.astype(jnp.int32))
    group = at >> 3
    row = jnp.where(group < 9, at & 7, -1000)
    taps = [jnp.zeros((ch, width), F32) for _ in range(3)]
    for a in range(3):
        for c in range(3):
            inside = group == a * 3 + c
            for b in range(3):
                k = tap(a, b, c, flip)
                taps[b] = jnp.where(inside, w[:, k : k + 1], taps[b])
    one = 9 * SLAB
    start = jnp.zeros((ch, width), F32)
    if bias is not None:
        start = jnp.where((q == one) | (q == 2 * part + one), bias, start)
    for j in range(BLOCK):
        acc = start
        for b in range(3):
            acc = jnp.where(row == j + b, taps[b], acc)
        hi = acc.astype(BF16).astype(F32)
        out_ref[j * ch : (j + 1) * ch, :] = jnp.where(low, acc - hi, hi).astype(BF16)


def build_spread(w, out_ref, flip):
    ch = w.shape[0]
    rows, width = out_ref.shape[0] // 2, out_ref.shape[1]
    n = w.shape[1]

    def place(shape):
        i = iota(shape, 0)
        ac = (i * 43) >> 8
        a = (ac * 11) >> 5
        return ac, 9 * a + (ac - 3 * a), i - BLOCK * ac

    ac, k0, _ = place((rows, n))
    kid = iota((rows, n), 1)
    _, _, r = place((rows, width))
    lane = iota((rows, width), 1)
    col = jnp.zeros((rows, width), jnp.int32)
    for i in range(1, SLAB):
        col = col + (lane >= i * ch).astype(jnp.int32)
    parts = halves(jnp.concatenate([w] * SLAB, axis=0))
    accs = [jnp.zeros((rows, width), F32) for _ in parts]
    for b in range(3):
        k = k0 + 3 * b
        if flip:
            k = n - 1 - k
        pick = jnp.where((kid == k) & (ac < 9), 1.0, 0.0).astype(BF16)
        for i, part in enumerate(parts):
            value = lax.dot_general(pick, part, (((1,), (1,)), ((), ())), preferred_element_type=F32)
            accs[i] = jnp.where(col - r == b, value, accs[i])
    out_ref[...] = jnp.concatenate(accs, axis=0).astype(BF16)


def sizes(L):
    nb = -(-(L + 10) // BLOCK)
    mb = -(-(L + 8) // BLOCK)
    gb = -(-(L + 4) // BLOCK)
    return nb, mb, gb, L + 6, L + 8, up(BLOCK * gb, 8)


def kernel(
    n_t, n_l, D, L, C, S,
    x_ref, y_ref, m_ref, land_ref, *rest,
):
    weights, out_ref, filled = rest[:7], rest[7], rest[8:15]
    kernel_body(
        n_t, n_l, D, L, C, S, x_ref, y_ref, m_ref, land_ref, weights, filled, out_ref, *rest[15:]
    )


def kernel_body(
    n_t, n_l, D, L, C, S,
    x_ref, y_ref, m_ref, land_ref, weights, filled, out_ref,
    xr, yr, mr, lr, xh, xl, mh, ml, hid, rem, bid, bem, pb, qb, mis_ref, gf, g3, hraw, h3, cell,
    te, td, sd, se, gwt, wst, gst,
    send, recv, local,
):
    N = x_ref.shape[-1]
    R = L + 2 * SLOT
    NB, MB, GB, BH, MR, GR = sizes(L)
    WG, WS = gwt.shape[2], wst.shape[1]
    KG = gf.shape[1]
    total = n_t * D
    W = min(total, D + 2 * HALO_DAYS)
    HALF = D // 2
    t = lax.axis_index("tm")
    l = lax.axis_index("lon")
    right = lax.rem(l + 1, n_l)
    left = lax.rem(l + n_l - 1, n_l)
    pairs = n_t == 2

    def window(tt):
        return 0 if W == total else jnp.clip(tt * D - HALO_DAYS, 0, total - W)

    o = t * D - window(t)

    own = pl.ds(SLOT, L)
    ew_ref, eb_ref, dw_ref, db_ref, gw_ref, gb_ref, ow_ref = filled

    barrier = pltpu.get_barrier_semaphore()
    if pairs:
        moves = [(2, -1), (2, 1), (0, -1), (0, 1), (2, 0)]
    else:
        moves = [(dt, dl) for dt in (-1, 1, 0) for dl in (-1, 1, 0) if (dt, dl) != (0, 0)]

    def group(dt, sign=1):
        return 1 - t if dt == 2 else t + sign * dt

    def target(dt, dl):
        return (group(dt), {-1: left, 0: l, 1: right}[dl])

    def guarded(dt, fn):
        if dt == 0 or pairs:
            fn()
        else:
            pl.when((t + dt >= 0) & (t + dt < n_t))(fn)

    for dt, dl in moves:
        def greet(dt=dt, dl=dl):
            pl.semaphore_signal(barrier, inc=1, device_id=target(dt, dl), device_id_type=MESH)
        guarded(dt, greet)

    tiles = [
        pltpu.make_async_copy(x_ref, xr.at[0, pl.ds(o, D), own, :], local.at[7]),
        pltpu.make_async_copy(y_ref, yr.at[:, own, :], local.at[8]),
        pltpu.make_async_copy(m_ref, mr.at[:, own, :], local.at[9]),
        pltpu.make_async_copy(land_ref, lr.at[own, :], local.at[10]),
    ]

    if n_t > 2:
        xr[...] = jnp.zeros_like(xr)
    for copy in tiles:
        copy.start()
    fetches = [
        pltpu.make_async_copy(a, b, local.at[i]) for i, (a, b) in enumerate(zip(weights, filled))
    ]
    for copy in fetches:
        copy.start()

    def src_lon(dl):
        return {-1: pl.ds(0, SLOT), 0: pl.ds(0, L), 1: pl.ds(L - SLOT, SLOT)}[dl]

    def own_lon(dl):
        lon = src_lon(dl)
        return pl.ds(SLOT + lon.start, lon.size)

    def dst_lon(dl):
        return {-1: pl.ds(SLOT + L, SLOT), 0: pl.ds(SLOT, L), 1: pl.ds(0, SLOT)}[dl]

    def x_copy(it, src, base_day, base_lon, dt, dl, index, sender):
        if dt == 2:
            first = (1 - sender) * (D - HALO_DAYS)
            goal = 0
        else:
            first = D - HALO_DAYS if dt == 1 else 0
            goal = window(sender + dt)
        days = D if dt == 0 else HALO_DAYS
        day = sender * D + first - goal
        lon = src_lon(dl)
        source = src.at[pl.ds(base_day + first, days), pl.ds(base_lon + lon.start, lon.size), :]
        return pltpu.make_async_remote_copy(
            src_ref=source,
            dst_ref=xr.at[it, pl.ds(day, days), dst_lon(dl), :],
            send_sem=send.at[index], recv_sem=recv.at[index],
            device_id=target(dt, dl), device_id_type=MESH,
        )

    def plain_copy(src, dst, dl, index):
        return pltpu.make_async_remote_copy(
            src_ref=src, dst_ref=dst, send_sem=send.at[index], recv_sem=recv.at[index],
            device_id=target(0, dl), device_id_type=MESH,
        )

    def x_start(it, src, base_day, base_lon, slot0):
        for i, (dt, dl) in enumerate(moves):
            def go(i=i, dt=dt, dl=dl):
                x_copy(it, src, base_day, base_lon, dt, dl, slot0 + i, t).start()
            guarded(dt, go)

    def x_wait(it, src, base_day, base_lon, slot0, straight):
        for i, (dt, dl) in enumerate(moves):
            if (dl == 0) != straight:
                continue
            def got(i=i, dt=dt, dl=dl):
                x_copy(it, src, base_day, base_lon, dt, dl, slot0 + i, group(dt, -1)).wait_recv()
            def sent(i=i, dt=dt, dl=dl):
                x_copy(it, src, base_day, base_lon, dt, dl, slot0 + i, t).wait_send()
            guarded(-dt, got)
            guarded(dt, sent)

    first_slot, next_slot, other_slot = 0, len(moves), 2 * len(moves)
    for copy in tiles:
        copy.wait()
    if pairs:
        around = 5
    else:
        around = 2 + 3 * ((t > 0).astype(jnp.int32) + (t < n_t - 1).astype(jnp.int32))
    pl.semaphore_wait(barrier, around)

    x_start(0, xr.at[0], o, SLOT, first_slot)
    others = []
    for i, dl in enumerate((-1, 1)):
        at = other_slot + 3 * i
        others.append(plain_copy(yr.at[:, own_lon(dl), :], yr.at[:, dst_lon(dl), :], dl, at))
        others.append(plain_copy(mr.at[:, own_lon(dl), :], mr.at[:, dst_lon(dl), :], dl, at + 1))
        others.append(plain_copy(lr.at[own_lon(dl), :], lr.at[dst_lon(dl), :], dl, at + 2))
    for copy in others:
        copy.start()

    for ref in (mh, ml):
        ref[...] = jnp.zeros_like(ref)
    for ref in (xh, xl, pb, qb):
        for day in (0, W + 1):
            ref[day] = jnp.zeros(ref.shape[1:], F32)
    if xh.shape[2] > R:
        for ref in (xh, xl):
            ref[:, :, R:, :] = jnp.zeros((W + 2, 3, xh.shape[2] - R, N), F32)
    h3[D * (L + 2) * 3 * S :, :] = jnp.zeros((h3.shape[0] - D * (L + 2) * 3 * S, N), BF16)
    ones = (iota((KG - 3 * GR, N), 0) < 3).astype(F32)
    for d in range(D):
        gf[d, 0 : 3 * GR, :] = jnp.zeros((3 * GR, N), F32)
        gf[d, 3 * GR :, :] = ones

    for copy in fetches:
        copy.wait()
    ew, dw = ew_ref[...], dw_ref[...]
    build_lift(ew, column(eb_ref[...]), te, False)
    build_spread(dw, sd, False)
    build_lift(dw, None, td, True)
    build_spread(ew, se, True)

    wide = gw_ref[...].astype(F32)
    gate_rows = iota((4 * S, 1), 0)
    scale = jnp.where((gate_rows >= 2 * S) & (gate_rows < 3 * S), 1.0, 0.5)
    wide = wide * scale
    gbias = column(gb_ref[...]) * scale
    b_hi = gbias.astype(BF16)
    b_rest = gbias - b_hi.astype(F32)
    b_mid = b_rest.astype(BF16).astype(F32)
    b_low = b_rest - b_mid
    ins = S + 1
    q = iota((4 * S, WG), 1)
    start = jnp.where(q == 3 * GR, b_hi.astype(F32), 0.0)
    start = jnp.where(q == 3 * GR + 1, b_mid, start)
    start = jnp.where(q == 3 * GR + 2, b_low, start)
    row = jnp.full((4 * S, WG), -1000, jnp.int32)
    taps = [jnp.zeros((4 * S, WG), F32) for _ in range(3)]
    for c in range(3):
        inside = (q >= c * GR) & (q < (c + 1) * GR)
        row = jnp.where(inside, q - c * GR, row)
        for b in range(3):
            k = (3 * b + c) * ins
            taps[b] = jnp.where(inside, wide[:, k : k + 1], taps[b])
    for j in range(L + 2):
        acc = start
        for b in range(3):
            acc = jnp.where(row == j + b, taps[b], acc)
        gwt[j] = acc.astype(BF16)

    for base in range(0, WS, 128):
        src = iota((9 * ins, 128), 0)
        lane = iota((9 * ins, 128), 1) + base
        want = lane + 1
        for i in range(1, 9):
            want = want + (lane >= i * S).astype(jnp.int32)
        pick = ((src == want) & (lane < 9 * S)).astype(F32).astype(BF16)
        wst[:, base : base + 128] = mm((0.5 * wide).astype(BF16), pick).astype(BF16)

    oweight = jnp.broadcast_to(0.5 * column(ow_ref[...]), (S, 2 * N))
    dbias = db_ref[0]

    def finish(parts):
        lower, mid, upper = parts
        lane = iota(lower.shape, 1)
        return (
            jnp.where(lane == 0, 0.0, pltpu.roll(lower, 1, 1))
            + mid
            + jnp.where(lane == N - 1, 0.0, pltpu.roll(upper, N - 1, 1))
        )

    def gather_taps(ref, d, i):
        parts = []
        for c in range(3):
            rows = [pl.ds((3 * a + c) * BLOCK, BLOCK) for a in range(3)]
            parts.append(ref[d, i, rows[0], :] + ref[d + 1, i, rows[1], :] + ref[d + 2, i, rows[2], :])
        return finish(parts)

    def planes(ref, d, n, rows):
        return [
            jnp.concatenate([ref[d + a + q, c, rows, :] for q in range(n)], axis=1)
            for a in range(3)
            for c in range(3)
        ]

    def span(radius):
        n = D + radius if pairs else min(W, D + 2 * radius)
        n = min(W, n)
        return (0 if n == W else jnp.clip(o - radius, 0, W - n)), n

    def groups(start, n):
        return [(start + k, min(2, n - k)) for k in range(0, n, 2)]

    def spread(weight, hidden, rest, size, count, out, d, n):
        rows = weight.shape[0] // 2
        for i in range(count):
            at = slice(i * BLOCK * C, min((i * BLOCK + SLAB) * C, size))
            k = at.stop - at.start
            sums = mm(weight[:, 0:k], hidden(at))
            sums = sums[0:rows] + sums[rows:] + mm(weight[0 : up(rows, 16), 0:k], rest(at))[0:rows]
            for q in range(n):
                out[d + q + 1, i] = sums[:, q * N : (q + 1) * N]

    def lift(weight, hi_ref, lo_ref, d, n, first, extra):
        rows = pl.ds(first, SLAB)
        hi = jnp.concatenate(planes(hi_ref, d, n, rows) + [extra[:, 0 : n * N]], axis=0).astype(BF16)
        lo = jnp.concatenate(planes(lo_ref, d, n, rows) + [blank[:, 0 : n * N]], axis=0).astype(BF16)
        pad = jnp.zeros((weight.shape[1] - 30 * SLAB, n * N), BF16)
        return mm(weight, jnp.concatenate([hi, lo, hi, pad], axis=0))

    unit = (iota((SLAB, 2 * N), 0) == 0).astype(F32)
    blank = jnp.zeros((SLAB, 2 * N), F32)

    s3, n3 = span(3)
    early = [i for i in range(NB) if BLOCK * i >= 6 and BLOCK * i + SLAB <= L + 6]
    late = [i for i in range(NB) if i not in early]

    def stage(it, first, rows):
        at = pl.ds(first, rows)
        for d in range(W):
            for c, v in enumerate(shifts(xr[it, d, at, :])):
                hi = v.astype(BF16).astype(F32)
                xh[d + 1, c, at, :] = hi
                xl[d + 1, c, at, :] = v - hi

    def encode(blocks):
        for d, n in groups(s3, n3):
            for i in blocks:
                enc = jnp.maximum(lift(te[...], xh, xl, d, n, SLOT - 6 + BLOCK * i, unit), 0.0)
                to = pl.ds(BLOCK * C * i, BLOCK * C)
                for ref, v in zip((hid, rem), halves(enc)):
                    for q in range(n):
                        ref[d + q, to, :] = v[:, q * N : (q + 1) * N]

    def begin(it):
        stage(it, SLOT, L)
        encode(early)

    def joined(ref, d, n):
        return lambda at: jnp.concatenate([ref[d + q, at, :] for q in range(n)], axis=1)

    def gradient(it, land=(), seas=()):
        stage(it, 0, SLOT)
        stage(it, SLOT + L, SLOT)
        encode(late)
        for d, n in groups(s3, n3):
            spread(sd, joined(hid, d, n), joined(rem, d, n), NB * BLOCK * C, MB, pb, d, n)

        for copy in land:
            copy.wait()
        s2, n2 = span(2)
        for k in range(n2):
            d = s2 + k
            for i in range(MB):
                at = pl.ds(SLOT - 4 + BLOCK * i, BLOCK)
                rebuilt = gather_taps(pb, d, i) + dbias
                mis = lr[at, :].astype(F32) * (xr[it, d, at, :] - rebuilt)
                to = pl.ds(BLOCK * i, BLOCK)
                mis_ref[d, to, :] = mis
                for c, v in enumerate(shifts(mis)):
                    hi = v.astype(BF16).astype(F32)
                    mh[d + 1, c, to, :] = hi
                    ml[d + 1, c, to, :] = v - hi

        s1, n1 = span(1)
        for d, n in groups(s1, n1):
            on = joined(hid, d, n)
            for i in range(-(-BH // BLOCK)):
                count = min(BLOCK, BH - BLOCK * i) * C
                lifted = lift(td[0:count, :], mh, ml, d, n, BLOCK * i, blank)
                at = (2 + BLOCK * i) * C
                live = on(slice(at, at + count)) > jnp.zeros((), BF16)
                for ref, v in zip((bid, bem), halves(lifted)):
                    v = jnp.where(live, v, jnp.zeros((), BF16))
                    for q in range(n):
                        ref[d + q, BLOCK * C * i : BLOCK * C * i + count, :] = v[:, q * N : (q + 1) * N]
        for d, n in groups(s1, n1):
            spread(se, joined(bid, d, n), joined(bem, d, n), BH * C, GB, qb, d, n)

        for copy in seas:
            copy.wait()
        for k in range(D):
            d = o + k
            for i in range(GB):
                at = pl.ds(SLOT - 2 + BLOCK * i, BLOCK)
                seen = mr[k, at, :].astype(F32)
                grad = (
                    2.0 * seen * (xr[it, d, at, :] - yr[k, at, :])
                    + mis_ref[d, pl.ds(2 + BLOCK * i, BLOCK), :]
                    - gather_taps(qb, d, i)
                )
                for c, v in enumerate(shifts(grad)):
                    gf[k, pl.ds(c * GR + BLOCK * i, BLOCK), :] = v
        for p in range(HALF):
            v = jnp.concatenate([gf[2 * p], gf[2 * p + 1]], axis=1).astype(BF16)
            g3[p, 0:KG, :] = v
            if WG > KG:
                g3[p, KG:, :] = jnp.zeros((WG - KG, 2 * N), BF16)

    def twice(v):
        return jnp.tanh(v) + 1.0

    def put_h3(d, lon, h):
        v = jnp.concatenate(list(shifts(h)), axis=0).astype(BF16)
        h3[pl.ds(pl.multiple_of((d * (L + 2) + lon) * 3 * S, 16), 3 * S), :] = v

    x_wait(0, xr.at[0], o, SLOT, first_slot, True)
    begin(0)
    x_wait(0, xr.at[0], o, SLOT, first_slot, False)
    gradient(0, others[2::3], others[0::3] + others[1::3])

    def first_gates(j, inside):
        for p in range(HALF):
            rhs = g3[p]
            up_ = mm(gwt[j, 0:S, :], rhs)
            rest = mm(gwt[j, 2 * S : 4 * S, :], rhs)
            state = 0.5 * (twice(up_) * jnp.tanh(rest[0:S]))
            hidden = twice(rest[S : 2 * S]) * jnp.tanh(state)
            if inside:
                cell[j - 1, p] = state
                step = jnp.sum(oweight * hidden, axis=0, keepdims=True)
            for i in range(2):
                d = 2 * p + i
                hraw[d, j] = hidden[:, i * N : (i + 1) * N]
                if inside:
                    at = pl.ds(SLOT - 1 + j, 1)
                    xr[1, o + d, at, :] = xr[0, o + d, at, :] - step[:, i * N : (i + 1) * N]

    def inner(j, carry):
        first_gates(j, True)
        return carry

    lax.fori_loop(1, L + 1, inner, 0, unroll=8)
    x_start(1, xr.at[1], o, SLOT, next_slot)
    first_gates(0, False)
    first_gates(L + 1, False)

    def place(j, carry):
        for d in range(D):
            put_h3(d, j, hraw[d, j])
        return carry

    lax.fori_loop(0, L + 2, place, 0, unroll=2)

    def state_part(j, carry):
        for p in range(HALF):
            rhs = jnp.concatenate(
                [
                    h3[pl.ds(pl.multiple_of(((2 * p + i) * (L + 2) + j) * 3 * S, 16), WS), :]
                    for i in range(2)
                ],
                axis=1,
            )
            gst[j, p] = mm(wst[...], rhs)
        return carry

    lax.fori_loop(0, L, state_part, 0, unroll=2)
    x_wait(1, xr.at[1], o, SLOT, next_slot, True)
    begin(1)
    x_wait(1, xr.at[1], o, SLOT, next_slot, False)
    gradient(1)

    def last_gates(j, carry):
        for p in range(HALF):
            sums = gst[j, p] + mm(gwt[j + 1], g3[p])
            state = twice(sums[S : 2 * S]) * cell[j, p] + twice(sums[0:S]) * jnp.tanh(
                sums[2 * S : 3 * S]
            )
            hidden = twice(sums[3 * S :]) * jnp.tanh(0.5 * state)
            step = jnp.sum(oweight * hidden, axis=0, keepdims=True)
            for i in range(2):
                d = 2 * p + i
                out_ref[d, pl.ds(j, 1), :] = (
                    xr[1, o + d, pl.ds(SLOT + j, 1), :] - step[:, i * N : (i + 1) * N]
                )
        return carry

    lax.fori_loop(0, L, last_gates, 0, unroll=8)


def body(n_t, n_l, x, y, m, land, ew, eb, dw, db, gw, gb, ow):
    D, L, N = x.shape[1:]
    C = eb.shape[0]
    S = ow.shape[0]
    R = L + 2 * SLOT
    NB, MB, GB, BH, MR, GR = sizes(L)
    W = min(n_t * D, D + 2 * HALO_DAYS)
    RX = max(R, up(BLOCK * NB + 4, 8))
    RM = up(max(BLOCK * MB, BLOCK * (-(-BH // BLOCK) - 1) + SLAB), 8)
    taps = up(9 * BLOCK, 8)
    KG = up(3 * GR + 3, 16)
    WE, WG, WS = up(30 * SLAB, 128), up(KG, 128), up(9 * S, 128)
    G = 4 * S
    copies = 2 * (5 if n_t == 2 else 8) + 6
    vm = pltpu.VMEM
    scratch = [
        vm((2, W, R, N), F32), vm((D, R, N), F32), vm((D, R, N), jnp.int32), vm((R, N), jnp.int32),
        vm((W + 2, 3, RX, N), F32), vm((W + 2, 3, RX, N), F32),
        vm((W + 2, 3, RM, N), F32), vm((W + 2, 3, RM, N), F32),
        vm((W, NB * BLOCK * C, N), BF16), vm((W, NB * BLOCK * C, N), BF16),
        vm((W, BH * C, N), BF16), vm((W, BH * C, N), BF16), vm((W + 2, MB, taps, N), F32), vm((W + 2, GB, taps, N), F32),
        vm((W, RM, N), F32), vm((D, KG, N), F32), vm((D // 2, WG, 2 * N), BF16), vm((D, L + 2, S, N), F32),
        vm((D * (L + 2) * 3 * S + WS - 9 * S, N), BF16), vm((L, D // 2, S, 2 * N), F32),
        vm((BLOCK * C, WE), BF16), vm((BLOCK * C, WE), BF16),
        vm((2 * taps, SLAB * C), BF16), vm((2 * taps, SLAB * C), BF16),
        vm((L + 2, G, WG), BF16), vm((G, WS), BF16), vm((L, D // 2, G, 2 * N), F32),
        pltpu.SemaphoreType.DMA((copies,)), pltpu.SemaphoreType.DMA((copies,)),
        pltpu.SemaphoreType.DMA((11,)),
    ]
    v = pl.BlockSpec(memory_space=pltpu.VMEM)
    whole = pl.BlockSpec(memory_space=pltpu.HBM)
    weights = (ew, eb[None], dw, db, gw, gb[None], ow[None])
    scratch = [(pltpu.SMEM if w is db else vm)(w.shape, w.dtype) for w in weights] + scratch
    out = pl.pallas_call(
        functools.partial(kernel, n_t, n_l, D, L, C, S),
        out_shape=pltpu.VMEM((D, L, N), F32),
        in_specs=[whole] * 11,
        out_specs=v,
        scratch_shapes=scratch,
        compiler_params=pltpu.CompilerParams(
            collective_id=0, has_side_effects=True, vmem_limit_bytes=67000000
        ),
        name="solver",
    )(x[0], y[0], m[0], land, *weights)
    return out[None]


def solution(mesh):
    tile = P(None, "tm", "lon", None)
    run = functools.partial(body, mesh.shape["tm"], mesh.shape["lon"])
    return jax.shard_map(
        run, mesh=mesh, in_specs=(tile, tile, tile, P("lon", None)) + (P(),) * 7,
        out_specs=tile, check_vma=False,
    )
```

```python
import functools

import jax
import jax.numpy as jnp
from jax import lax
from jax.experimental import pallas as pl
from jax.experimental.pallas import tpu as pltpu
from jax.sharding import PartitionSpec as P

SOLVER_ITERS = 2
HALO_DAYS = 4
SLOT = 8
BLOCK = 6
SLAB = 8
MESH = pl.DeviceIdType.MESH
F32, BF16 = jnp.float32, jnp.bfloat16


def up(n, m):
    return (n + m - 1) // m * m


def iota(shape, dim):
    return lax.broadcasted_iota(jnp.int32, shape, dim)


def halves(v):
    hi = v.astype(BF16)
    return hi, (v - hi.astype(F32)).astype(BF16)


def mm(a, b):
    return jnp.dot(a, b, preferred_element_type=F32)


def column(row):
    n = row.shape[1]
    eye = iota((n, n), 0) == iota((n, n), 1)
    return jnp.sum(jnp.where(eye, jnp.broadcast_to(row, (n, n)), 0.0), axis=1, keepdims=True)


def shifts(v):
    lanes = v.shape[-1]
    lane = iota(v.shape, v.ndim - 1)
    lower = jnp.where(lane == 0, 0.0, pltpu.roll(v, 1, v.ndim - 1))
    upper = jnp.where(lane == lanes - 1, 0.0, pltpu.roll(v, lanes - 1, v.ndim - 1))
    return lower, v, upper


def tap(a, b, c, flip):
    k = 9 * a + 3 * b + c
    return 26 - k if flip else k


def build_lift(w, bias, out_ref, flip, turn):
    ch = w.shape[0]
    width = out_ref.shape[1]
    part = 10 * SLAB
    q = iota((ch, width), 1)
    low = q >= 2 * part
    at = q - part * ((q >= part).astype(jnp.int32) + low.astype(jnp.int32))
    group = at >> 3
    row = jnp.where(group < 9, at & 7, -1000)
    taps = [jnp.zeros((ch, width), F32) for _ in range(3)]
    for a in range(3):
        for c in range(3):
            inside = group == (a + turn * (2 - 2 * a)) * 3 + c
            for b in range(3):
                k = tap(a, b, c, flip)
                taps[b] = jnp.where(inside, w[:, k : k + 1], taps[b])
    one = 9 * SLAB
    start = jnp.zeros((ch, width), F32)
    if bias is not None:
        start = jnp.where((q == one) | (q == 2 * part + one), bias, start)
    for j in range(BLOCK):
        acc = start
        for b in range(3):
            acc = jnp.where(row == j + b, taps[b], acc)
        hi = acc.astype(BF16).astype(F32)
        out_ref[j * ch : (j + 1) * ch, :] = jnp.where(low, acc - hi, hi).astype(BF16)


def build_spread(w, out_ref, flip, turn):
    ch = w.shape[0]
    rows, width = out_ref.shape[0] // 2, out_ref.shape[1]
    n = w.shape[1]

    def place(shape):
        i = iota(shape, 0)
        ac = (i * 43) >> 8
        a = (ac * 11) >> 5
        return ac, 9 * (a + turn * (2 - 2 * a)) + (ac - 3 * a), i - BLOCK * ac

    ac, k0, _ = place((rows, n))
    kid = iota((rows, n), 1)
    _, _, r = place((rows, width))
    lane = iota((rows, width), 1)
    col = jnp.zeros((rows, width), jnp.int32)
    for i in range(1, SLAB):
        col = col + (lane >= i * ch).astype(jnp.int32)
    parts = halves(jnp.concatenate([w] * SLAB, axis=0))
    accs = [jnp.zeros((rows, width), F32) for _ in parts]
    for b in range(3):
        k = k0 + 3 * b
        if flip:
            k = n - 1 - k
        pick = jnp.where((kid == k) & (ac < 9), 1.0, 0.0).astype(BF16)
        for i, part in enumerate(parts):
            value = lax.dot_general(pick, part, (((1,), (1,)), ((), ())), preferred_element_type=F32)
            accs[i] = jnp.where(col - r == b, value, accs[i])
    out_ref[...] = jnp.concatenate(accs, axis=0).astype(BF16)


def sizes(L):
    nb = -(-(L + 10) // BLOCK)
    mb = -(-(L + 8) // BLOCK)
    gb = -(-(L + 4) // BLOCK)
    return nb, mb, gb, L + 6, L + 8, up(BLOCK * gb, 8)


def kernel(
    n_t, n_l, D, L, C, S,
    x_ref, y_ref, m_ref, land_ref, *rest,
):
    weights, out_ref, filled = rest[:7], rest[7], rest[8:15]
    kernel_body(
        n_t, n_l, D, L, C, S, x_ref, y_ref, m_ref, land_ref, weights, filled, out_ref, *rest[15:]
    )


def kernel_body(
    n_t, n_l, D, L, C, S,
    x_ref, y_ref, m_ref, land_ref, weights, filled, out_ref,
    xr, yr, mr, lr, xh, xl, mh, ml, hid, rem, bid, bem, pb, qb, mis_ref, gf, g3, hraw, h3, cell,
    te, td, sd, se, gwt, wst, gst,
    send, recv, local,
):
    N = x_ref.shape[-1]
    R = L + 2 * SLOT
    NB, MB, GB, BH, MR, GR = sizes(L)
    WG, WS = gwt.shape[2], wst.shape[1]
    KG = gf.shape[1]
    total = n_t * D
    W = min(total, D + 2 * HALO_DAYS)
    HALF = D // 2
    t = lax.axis_index("tm")
    l = lax.axis_index("lon")
    right = lax.rem(l + 1, n_l)
    left = lax.rem(l + n_l - 1, n_l)
    pairs = n_t == 2
    turn = t if pairs else 0

    def window(tt):
        return 0 if W == total else jnp.clip(tt * D - HALO_DAYS, 0, total - W)

    o = t * D - window(t)

    own = pl.ds(SLOT, L)
    home = 0 if pairs else o

    def actual(k):
        return k + turn * (W - 1 - 2 * k)

    def mine(k):
        return k + turn * (D - 1 - 2 * k)

    ew_ref, eb_ref, dw_ref, db_ref, gw_ref, gb_ref, ow_ref = filled

    barrier = pltpu.get_barrier_semaphore()
    if pairs:
        moves = [(2, -1), (2, 1), (0, -1), (0, 1), (2, 0)]
    else:
        moves = [(dt, dl) for dt in (-1, 1, 0) for dl in (-1, 1, 0) if (dt, dl) != (0, 0)]

    def group(dt, sign=1):
        return 1 - t if dt == 2 else t + sign * dt

    def target(dt, dl):
        return (group(dt), {-1: left, 0: l, 1: right}[dl])

    def guarded(dt, fn):
        if dt == 0 or pairs:
            fn()
        else:
            pl.when((t + dt >= 0) & (t + dt < n_t))(fn)

    for dt, dl in moves:
        def greet(dt=dt, dl=dl):
            pl.semaphore_signal(barrier, inc=1, device_id=target(dt, dl), device_id_type=MESH)
        guarded(dt, greet)

    tiles = [
        pltpu.make_async_copy(x_ref, xr.at[0, pl.ds(o, D), own, :], local.at[7]),
        pltpu.make_async_copy(y_ref, yr.at[:, own, :], local.at[8]),
        pltpu.make_async_copy(m_ref, mr.at[:, own, :], local.at[9]),
        pltpu.make_async_copy(land_ref, lr.at[own, :], local.at[10]),
    ]

    if n_t > 2:
        xr[...] = jnp.zeros_like(xr)
    for copy in tiles:
        copy.start()
    fetches = [
        pltpu.make_async_copy(a, b, local.at[i]) for i, (a, b) in enumerate(zip(weights, filled))
    ]
    for copy in fetches:
        copy.start()

    def src_lon(dl):
        return {-1: pl.ds(0, SLOT), 0: pl.ds(0, L), 1: pl.ds(L - SLOT, SLOT)}[dl]

    def own_lon(dl):
        lon = src_lon(dl)
        return pl.ds(SLOT + lon.start, lon.size)

    def dst_lon(dl):
        return {-1: pl.ds(SLOT + L, SLOT), 0: pl.ds(SLOT, L), 1: pl.ds(0, SLOT)}[dl]

    def x_copy(it, src, base_day, base_lon, dt, dl, index, sender):
        if dt == 2:
            first = (1 - sender) * (D - HALO_DAYS)
            goal = 0
        else:
            first = D - HALO_DAYS if dt == 1 else 0
            goal = window(sender + dt)
        days = D if dt == 0 else HALO_DAYS
        day = sender * D + first - goal
        lon = src_lon(dl)
        source = src.at[pl.ds(base_day + first, days), pl.ds(base_lon + lon.start, lon.size), :]
        return pltpu.make_async_remote_copy(
            src_ref=source,
            dst_ref=xr.at[it, pl.ds(day, days), dst_lon(dl), :],
            send_sem=send.at[index], recv_sem=recv.at[index],
            device_id=target(dt, dl), device_id_type=MESH,
        )

    def plain_copy(src, dst, dl, index):
        return pltpu.make_async_remote_copy(
            src_ref=src, dst_ref=dst, send_sem=send.at[index], recv_sem=recv.at[index],
            device_id=target(0, dl), device_id_type=MESH,
        )

    def x_start(it, src, base_day, base_lon, slot0):
        for i, (dt, dl) in enumerate(moves):
            def go(i=i, dt=dt, dl=dl):
                x_copy(it, src, base_day, base_lon, dt, dl, slot0 + i, t).start()
            guarded(dt, go)

    def x_wait(it, src, base_day, base_lon, slot0, straight):
        for i, (dt, dl) in enumerate(moves):
            if (dl == 0) != straight:
                continue
            def got(i=i, dt=dt, dl=dl):
                x_copy(it, src, base_day, base_lon, dt, dl, slot0 + i, group(dt, -1)).wait_recv()
            def sent(i=i, dt=dt, dl=dl):
                x_copy(it, src, base_day, base_lon, dt, dl, slot0 + i, t).wait_send()
            guarded(-dt, got)
            guarded(dt, sent)

    first_slot, next_slot, other_slot = 0, len(moves), 2 * len(moves)
    for copy in tiles:
        copy.wait()
    if pairs:
        around = 5
    else:
        around = 2 + 3 * ((t > 0).astype(jnp.int32) + (t < n_t - 1).astype(jnp.int32))
    pl.semaphore_wait(barrier, around)

    x_start(0, xr.at[0], o, SLOT, first_slot)
    others = []
    for i, dl in enumerate((-1, 1)):
        at = other_slot + 3 * i
        others.append(plain_copy(yr.at[:, own_lon(dl), :], yr.at[:, dst_lon(dl), :], dl, at))
        others.append(plain_copy(mr.at[:, own_lon(dl), :], mr.at[:, dst_lon(dl), :], dl, at + 1))
        others.append(plain_copy(lr.at[own_lon(dl), :], lr.at[dst_lon(dl), :], dl, at + 2))
    for copy in others:
        copy.start()

    for ref in (mh, ml):
        ref[...] = jnp.zeros_like(ref)
    for ref in (xh, xl, pb, qb):
        for day in (0, W + 1):
            ref[day] = jnp.zeros(ref.shape[1:], F32)
    if xh.shape[2] > R:
        for ref in (xh, xl):
            ref[:, :, R:, :] = jnp.zeros((W + 2, 3, xh.shape[2] - R, N), F32)
    h3[D * (L + 2) * 3 * S :, :] = jnp.zeros((h3.shape[0] - D * (L + 2) * 3 * S, N), BF16)
    ones = (iota((KG - 3 * GR, N), 0) < 3).astype(F32)
    for d in range(D):
        gf[d, 0 : 3 * GR, :] = jnp.zeros((3 * GR, N), F32)
        gf[d, 3 * GR :, :] = ones

    for copy in fetches:
        copy.wait()
    ew, dw = ew_ref[...], dw_ref[...]
    build_lift(ew, column(eb_ref[...]), te, False, turn)
    build_spread(dw, sd, False, turn)
    build_lift(dw, None, td, True, turn)
    build_spread(ew, se, True, turn)

    wide = gw_ref[...].astype(F32)
    gate_rows = iota((4 * S, 1), 0)
    scale = jnp.where((gate_rows >= 2 * S) & (gate_rows < 3 * S), 1.0, 0.5)
    wide = wide * scale
    gbias = column(gb_ref[...]) * scale
    b_hi = gbias.astype(BF16)
    b_rest = gbias - b_hi.astype(F32)
    b_mid = b_rest.astype(BF16).astype(F32)
    b_low = b_rest - b_mid
    ins = S + 1
    q = iota((4 * S, WG), 1)
    start = jnp.where(q == 3 * GR, b_hi.astype(F32), 0.0)
    start = jnp.where(q == 3 * GR + 1, b_mid, start)
    start = jnp.where(q == 3 * GR + 2, b_low, start)
    row = jnp.full((4 * S, WG), -1000, jnp.int32)
    taps = [jnp.zeros((4 * S, WG), F32) for _ in range(3)]
    for c in range(3):
        inside = (q >= c * GR) & (q < (c + 1) * GR)
        row = jnp.where(inside, q - c * GR, row)
        for b in range(3):
            k = (3 * b + c) * ins
            taps[b] = jnp.where(inside, wide[:, k : k + 1], taps[b])
    for j in range(L + 2):
        acc = start
        for b in range(3):
            acc = jnp.where(row == j + b, taps[b], acc)
        gwt[j] = acc.astype(BF16)

    for base in range(0, WS, 128):
        src = iota((9 * ins, 128), 0)
        lane = iota((9 * ins, 128), 1) + base
        want = lane + 1
        for i in range(1, 9):
            want = want + (lane >= i * S).astype(jnp.int32)
        pick = ((src == want) & (lane < 9 * S)).astype(F32).astype(BF16)
        wst[:, base : base + 128] = mm((0.5 * wide).astype(BF16), pick).astype(BF16)

    oweight = jnp.broadcast_to(0.5 * column(ow_ref[...]), (S, 2 * N))
    dbias = db_ref[0]

    def finish(parts):
        lower, mid, upper = parts
        lane = iota(lower.shape, 1)
        return (
            jnp.where(lane == 0, 0.0, pltpu.roll(lower, 1, 1))
            + mid
            + jnp.where(lane == N - 1, 0.0, pltpu.roll(upper, N - 1, 1))
        )

    def gather_taps(ref, d, i):
        parts = []
        for c in range(3):
            rows = [pl.ds((3 * a + c) * BLOCK, BLOCK) for a in range(3)]
            parts.append(ref[d, i, rows[0], :] + ref[d + 1, i, rows[1], :] + ref[d + 2, i, rows[2], :])
        return finish(parts)

    def planes(ref, d, n, rows):
        return [
            jnp.concatenate([ref[d + a + q, c, rows, :] for q in range(n)], axis=1)
            for a in range(3)
            for c in range(3)
        ]

    def span(radius):
        n = D + radius if pairs else min(W, D + 2 * radius)
        n = min(W, n)
        return (0 if pairs or n == W else jnp.clip(o - radius, 0, W - n)), n

    def groups(start, n):
        return [(start + k, min(2, n - k)) for k in range(0, n, 2)]

    def spread(weight, hidden, rest, size, count, out, d, n):
        rows = weight.shape[0] // 2
        for i in range(count):
            at = slice(i * BLOCK * C, min((i * BLOCK + SLAB) * C, size))
            k = at.stop - at.start
            sums = mm(weight[:, 0:k], hidden(at))
            sums = sums[0:rows] + sums[rows:] + mm(weight[0 : up(rows, 16), 0:k], rest(at))[0:rows]
            for q in range(n):
                out[d + q + 1, i] = sums[:, q * N : (q + 1) * N]

    def lift(weight, hi_ref, lo_ref, d, n, first, extra):
        rows = pl.ds(first, SLAB)
        hi = jnp.concatenate(planes(hi_ref, d, n, rows) + [extra[:, 0 : n * N]], axis=0).astype(BF16)
        lo = jnp.concatenate(planes(lo_ref, d, n, rows) + [blank[:, 0 : n * N]], axis=0).astype(BF16)
        pad = jnp.zeros((weight.shape[1] - 30 * SLAB, n * N), BF16)
        return mm(weight, jnp.concatenate([hi, lo, hi, pad], axis=0))

    unit = (iota((SLAB, 2 * N), 0) == 0).astype(F32)
    blank = jnp.zeros((SLAB, 2 * N), F32)

    s3, n3 = span(3)
    early = [i for i in range(NB) if BLOCK * i >= 6 and BLOCK * i + SLAB <= L + 6]
    late = [i for i in range(NB) if i not in early]

    def stage(it, first, rows):
        at = pl.ds(first, rows)
        for d in range(W):
            for c, v in enumerate(shifts(xr[it, actual(d), at, :])):
                hi = v.astype(BF16).astype(F32)
                xh[d + 1, c, at, :] = hi
                xl[d + 1, c, at, :] = v - hi

    def encode(blocks):
        for d, n in groups(s3, n3):
            for i in blocks:
                enc = jnp.maximum(lift(te[...], xh, xl, d, n, SLOT - 6 + BLOCK * i, unit), 0.0)
                to = pl.ds(BLOCK * C * i, BLOCK * C)
                for ref, v in zip((hid, rem), halves(enc)):
                    for q in range(n):
                        ref[d + q, to, :] = v[:, q * N : (q + 1) * N]

    def begin(it):
        stage(it, SLOT, L)
        encode(early)

    def joined(ref, d, n):
        return lambda at: jnp.concatenate([ref[d + q, at, :] for q in range(n)], axis=1)

    def gradient(it):
        stage(it, 0, SLOT)
        stage(it, SLOT + L, SLOT)
        encode(late)
        for d, n in groups(s3, n3):
            spread(sd, joined(hid, d, n), joined(rem, d, n), NB * BLOCK * C, MB, pb, d, n)

        s2, n2 = span(2)
        for k in range(n2):
            d = s2 + k
            for i in range(MB):
                at = pl.ds(SLOT - 4 + BLOCK * i, BLOCK)
                rebuilt = gather_taps(pb, d, i) + dbias
                mis = lr[at, :].astype(F32) * (xr[it, actual(d), at, :] - rebuilt)
                to = pl.ds(BLOCK * i, BLOCK)
                mis_ref[d, to, :] = mis
                for c, v in enumerate(shifts(mis)):
                    hi = v.astype(BF16).astype(F32)
                    mh[d + 1, c, to, :] = hi
                    ml[d + 1, c, to, :] = v - hi

        s1, n1 = span(1)
        for d, n in groups(s1, n1):
            on = joined(hid, d, n)
            for i in range(-(-BH // BLOCK)):
                count = min(BLOCK, BH - BLOCK * i) * C
                lifted = lift(td[0:count, :], mh, ml, d, n, BLOCK * i, blank)
                at = (2 + BLOCK * i) * C
                live = on(slice(at, at + count)) > jnp.zeros((), BF16)
                for ref, v in zip((bid, bem), halves(lifted)):
                    v = jnp.where(live, v, jnp.zeros((), BF16))
                    for q in range(n):
                        ref[d + q, BLOCK * C * i : BLOCK * C * i + count, :] = v[:, q * N : (q + 1) * N]
        for d, n in groups(s1, n1):
            spread(se, joined(bid, d, n), joined(bem, d, n), BH * C, GB, qb, d, n)

        for k in range(D):
            d = home + k
            for i in range(GB):
                at = pl.ds(SLOT - 2 + BLOCK * i, BLOCK)
                seen = mr[mine(k), at, :].astype(F32)
                grad = (
                    2.0 * seen * (xr[it, actual(d), at, :] - yr[mine(k), at, :])
                    + mis_ref[d, pl.ds(2 + BLOCK * i, BLOCK), :]
                    - gather_taps(qb, d, i)
                )
                for c, v in enumerate(shifts(grad)):
                    gf[k, pl.ds(c * GR + BLOCK * i, BLOCK), :] = v
        for p in range(HALF):
            v = jnp.concatenate([gf[2 * p], gf[2 * p + 1]], axis=1).astype(BF16)
            g3[p, 0:KG, :] = v
            if WG > KG:
                g3[p, KG:, :] = jnp.zeros((WG - KG, 2 * N), BF16)

    def twice(v):
        return jnp.tanh(v) + 1.0

    def put_h3(d, lon, h):
        v = jnp.concatenate(list(shifts(h)), axis=0).astype(BF16)
        h3[pl.ds(pl.multiple_of((d * (L + 2) + lon) * 3 * S, 16), 3 * S), :] = v

    x_wait(0, xr.at[0], o, SLOT, first_slot, True)
    begin(0)
    for copy in others:
        copy.wait()
    x_wait(0, xr.at[0], o, SLOT, first_slot, False)
    gradient(0)

    def first_gates(j, inside):
        for p in range(HALF):
            rhs = g3[p]
            up_ = mm(gwt[j, 0:S, :], rhs)
            rest = mm(gwt[j, 2 * S : 4 * S, :], rhs)
            state = 0.5 * (twice(up_) * jnp.tanh(rest[0:S]))
            hidden = twice(rest[S : 2 * S]) * jnp.tanh(state)
            if inside:
                cell[j - 1, p] = state
                step = jnp.sum(oweight * hidden, axis=0, keepdims=True)
            for i in range(2):
                d = 2 * p + i
                hraw[d, j] = hidden[:, i * N : (i + 1) * N]
                if inside:
                    at = pl.ds(SLOT - 1 + j, 1)
                    to = actual(home + d)
                    xr[1, to, at, :] = xr[0, to, at, :] - step[:, i * N : (i + 1) * N]

    def inner(j, carry):
        first_gates(j, True)
        return carry

    lax.fori_loop(1, L + 1, inner, 0, unroll=8)
    x_start(1, xr.at[1], o, SLOT, next_slot)
    first_gates(0, False)
    first_gates(L + 1, False)

    def place(j, carry):
        for d in range(D):
            put_h3(d, j, hraw[d, j])
        return carry

    lax.fori_loop(0, L + 2, place, 0, unroll=2)

    def state_part(j, carry):
        for p in range(HALF):
            rhs = jnp.concatenate(
                [
                    h3[pl.ds(pl.multiple_of(((2 * p + i) * (L + 2) + j) * 3 * S, 16), WS), :]
                    for i in range(2)
                ],
                axis=1,
            )
            gst[j, p] = mm(wst[...], rhs)
        return carry

    lax.fori_loop(0, L, state_part, 0, unroll=2)
    x_wait(1, xr.at[1], o, SLOT, next_slot, True)
    begin(1)
    x_wait(1, xr.at[1], o, SLOT, next_slot, False)
    gradient(1)

    def last_gates(j, carry):
        for p in range(HALF):
            sums = gst[j, p] + mm(gwt[j + 1], g3[p])
            state = twice(sums[S : 2 * S]) * cell[j, p] + twice(sums[0:S]) * jnp.tanh(
                sums[2 * S : 3 * S]
            )
            hidden = twice(sums[3 * S :]) * jnp.tanh(0.5 * state)
            step = jnp.sum(oweight * hidden, axis=0, keepdims=True)
            for i in range(2):
                d = 2 * p + i
                out_ref[mine(d), pl.ds(j, 1), :] = (
                    xr[1, actual(home + d), pl.ds(SLOT + j, 1), :] - step[:, i * N : (i + 1) * N]
                )
        return carry

    lax.fori_loop(0, L, last_gates, 0, unroll=8)


def body(n_t, n_l, x, y, m, land, ew, eb, dw, db, gw, gb, ow):
    D, L, N = x.shape[1:]
    C = eb.shape[0]
    S = ow.shape[0]
    R = L + 2 * SLOT
    NB, MB, GB, BH, MR, GR = sizes(L)
    W = min(n_t * D, D + 2 * HALO_DAYS)
    RX = max(R, up(BLOCK * NB + 4, 8))
    RM = up(max(BLOCK * MB, BLOCK * (-(-BH // BLOCK) - 1) + SLAB), 8)
    taps = up(9 * BLOCK, 8)
    KG = up(3 * GR + 3, 16)
    WE, WG, WS = up(30 * SLAB, 128), up(KG, 128), up(9 * S, 128)
    G = 4 * S
    copies = 2 * (5 if n_t == 2 else 8) + 6
    vm = pltpu.VMEM
    scratch = [
        vm((2, W, R, N), F32), vm((D, R, N), F32), vm((D, R, N), jnp.int32), vm((R, N), jnp.int32),
        vm((W + 2, 3, RX, N), F32), vm((W + 2, 3, RX, N), F32),
        vm((W + 2, 3, RM, N), F32), vm((W + 2, 3, RM, N), F32),
        vm((W, NB * BLOCK * C, N), BF16), vm((W, NB * BLOCK * C, N), BF16),
        vm((W, BH * C, N), BF16), vm((W, BH * C, N), BF16), vm((W + 2, MB, taps, N), F32), vm((W + 2, GB, taps, N), F32),
        vm((W, RM, N), F32), vm((D, KG, N), F32), vm((D // 2, WG, 2 * N), BF16), vm((D, L + 2, S, N), F32),
        vm((D * (L + 2) * 3 * S + WS - 9 * S, N), BF16), vm((L, D // 2, S, 2 * N), F32),
        vm((BLOCK * C, WE), BF16), vm((BLOCK * C, WE), BF16),
        vm((2 * taps, SLAB * C), BF16), vm((2 * taps, SLAB * C), BF16),
        vm((L + 2, G, WG), BF16), vm((G, WS), BF16), vm((L, D // 2, G, 2 * N), F32),
        pltpu.SemaphoreType.DMA((copies,)), pltpu.SemaphoreType.DMA((copies,)),
        pltpu.SemaphoreType.DMA((11,)),
    ]
    v = pl.BlockSpec(memory_space=pltpu.VMEM)
    whole = pl.BlockSpec(memory_space=pltpu.HBM)
    weights = (ew, eb[None], dw, db, gw, gb[None], ow[None])
    scratch = [(pltpu.SMEM if w is db else vm)(w.shape, w.dtype) for w in weights] + scratch
    out = pl.pallas_call(
        functools.partial(kernel, n_t, n_l, D, L, C, S),
        out_shape=pltpu.VMEM((D, L, N), F32),
        in_specs=[whole] * 11,
        out_specs=v,
        scratch_shapes=scratch,
        compiler_params=pltpu.CompilerParams(
            collective_id=0, has_side_effects=True, vmem_limit_bytes=67000000
        ),
        name="solver",
    )(x[0], y[0], m[0], land, *weights)
    return out[None]


def solution(mesh):
    tile = P(None, "tm", "lon", None)
    run = functools.partial(body, mesh.shape["tm"], mesh.shape["lon"])
    return jax.shard_map(
        run, mesh=mesh, in_specs=(tile, tile, tile, P("lon", None)) + (P(),) * 7,
        out_specs=tile, check_vma=False,
    )
```

```python
import functools

import jax
import jax.numpy as jnp
from jax import lax
from jax.experimental import pallas as pl
from jax.experimental.pallas import tpu as pltpu
from jax.sharding import PartitionSpec as P

SOLVER_ITERS = 2
HALO_DAYS = 4
SLOT = 8
BLOCK = 6
SLAB = 8
SIDE = 6
MESH = pl.DeviceIdType.MESH
F32, BF16 = jnp.float32, jnp.bfloat16


def up(n, m):
    return (n + m - 1) // m * m


def iota(shape, dim):
    return lax.broadcasted_iota(jnp.int32, shape, dim)


def halves(v):
    hi = v.astype(BF16)
    return hi, (v - hi.astype(F32)).astype(BF16)


def mm(a, b):
    return jnp.dot(a, b, preferred_element_type=F32)


def column(row):
    n = row.shape[1]
    eye = iota((n, n), 0) == iota((n, n), 1)
    return jnp.sum(jnp.where(eye, jnp.broadcast_to(row, (n, n)), 0.0), axis=1, keepdims=True)


def shifts(v):
    lanes = v.shape[-1]
    lane = iota(v.shape, v.ndim - 1)
    lower = jnp.where(lane == 0, 0.0, pltpu.roll(v, 1, v.ndim - 1))
    upper = jnp.where(lane == lanes - 1, 0.0, pltpu.roll(v, lanes - 1, v.ndim - 1))
    return lower, v, upper


def tap(a, b, c, flip):
    k = 9 * a + 3 * b + c
    return 26 - k if flip else k


def build_lift(w, bias, out_ref, flip, turn):
    ch = w.shape[0]
    width = out_ref.shape[1]
    part = 10 * SLAB
    q = iota((ch, width), 1)
    low = q >= 2 * part
    at = q - part * ((q >= part).astype(jnp.int32) + low.astype(jnp.int32))
    group = at >> 3
    row = jnp.where(group < 9, at & 7, -1000)
    taps = [jnp.zeros((ch, width), F32) for _ in range(3)]
    for a in range(3):
        for c in range(3):
            inside = group == (a + turn * (2 - 2 * a)) * 3 + c
            for b in range(3):
                k = tap(a, b, c, flip)
                taps[b] = jnp.where(inside, w[:, k : k + 1], taps[b])
    one = 9 * SLAB
    start = jnp.zeros((ch, width), F32)
    if bias is not None:
        start = jnp.where((q == one) | (q == 2 * part + one), bias, start)
    for j in range(BLOCK):
        acc = start
        for b in range(3):
            acc = jnp.where(row == j + b, taps[b], acc)
        hi = acc.astype(BF16).astype(F32)
        out_ref[j * ch : (j + 1) * ch, :] = jnp.where(low, acc - hi, hi).astype(BF16)


def build_spread(w, out_ref, flip, turn):
    ch = w.shape[0]
    rows, width = out_ref.shape[0] // 2, out_ref.shape[1]
    n = w.shape[1]

    def place(shape):
        i = iota(shape, 0)
        ac = (i * 43) >> 8
        a = (ac * 11) >> 5
        return ac, 9 * (a + turn * (2 - 2 * a)) + (ac - 3 * a), i - BLOCK * ac

    ac, k0, _ = place((rows, n))
    kid = iota((rows, n), 1)
    _, _, r = place((rows, width))
    lane = iota((rows, width), 1)
    col = jnp.zeros((rows, width), jnp.int32)
    for i in range(1, SLAB):
        col = col + (lane >= i * ch).astype(jnp.int32)
    parts = halves(jnp.concatenate([w] * SLAB, axis=0))
    accs = [jnp.zeros((rows, width), F32) for _ in parts]
    for b in range(3):
        k = k0 + 3 * b
        if flip:
            k = n - 1 - k
        pick = jnp.where((kid == k) & (ac < 9), 1.0, 0.0).astype(BF16)
        for i, part in enumerate(parts):
            value = lax.dot_general(pick, part, (((1,), (1,)), ((), ())), preferred_element_type=F32)
            accs[i] = jnp.where(col - r == b, value, accs[i])
    out_ref[...] = jnp.concatenate(accs, axis=0).astype(BF16)


def sizes(L):
    nb = -(-(L + 10) // BLOCK)
    mb = -(-(L + 8) // BLOCK)
    gb = -(-(L + 4) // BLOCK)
    return nb, mb, gb, L + 6, L + 8, up(BLOCK * gb, 8)


def kernel(
    n_t, n_l, D, L, C, S,
    x_ref, y_ref, m_ref, land_ref, *rest,
):
    weights, out_ref, filled = rest[:7], rest[7], rest[8:15]
    kernel_body(
        n_t, n_l, D, L, C, S, x_ref, y_ref, m_ref, land_ref, weights, filled, out_ref, *rest[15:]
    )


def kernel_body(
    n_t, n_l, D, L, C, S,
    x_ref, y_ref, m_ref, land_ref, weights, filled, out_ref,
    xr, yr, mr, lr, xh, xl, mh, ml, hid, rem, bid, bem, pb, qb, mis_ref, gf, g3, hraw, h3, cell,
    te, td, sd, se, gwt, wst, gst,
    send, recv, local,
):
    N = x_ref.shape[-1]
    R = L + 2 * SLOT
    NB, MB, GB, BH, MR, GR = sizes(L)
    WG, WS = gwt.shape[2], wst.shape[1]
    KG = gf.shape[1]
    total = n_t * D
    W = min(total, D + 2 * HALO_DAYS)
    HALF = D // 2
    t = lax.axis_index("tm")
    l = lax.axis_index("lon")
    right = lax.rem(l + 1, n_l)
    left = lax.rem(l + n_l - 1, n_l)
    pairs = n_t == 2
    turn = t if pairs else 0

    def window(tt):
        return 0 if W == total else jnp.clip(tt * D - HALO_DAYS, 0, total - W)

    o = t * D - window(t)

    own = pl.ds(SLOT, L)
    home = 0 if pairs else o

    def actual(k):
        return k + turn * (W - 1 - 2 * k)

    def mine(k):
        return k + turn * (D - 1 - 2 * k)

    ew_ref, eb_ref, dw_ref, db_ref, gw_ref, gb_ref, ow_ref = filled

    barrier = pltpu.get_barrier_semaphore()
    if pairs:
        moves = [(2, -1), (2, 1), (0, -1), (0, 1), (2, 0)]
    else:
        moves = [(dt, dl) for dt in (-1, 1, 0) for dl in (-1, 1, 0) if (dt, dl) != (0, 0)]

    def group(dt, sign=1):
        return 1 - t if dt == 2 else t + sign * dt

    def target(dt, dl):
        return (group(dt), {-1: left, 0: l, 1: right}[dl])

    def guarded(dt, fn):
        if dt == 0 or pairs:
            fn()
        else:
            pl.when((t + dt >= 0) & (t + dt < n_t))(fn)

    for dt, dl in moves:
        def greet(dt=dt, dl=dl):
            pl.semaphore_signal(barrier, inc=1, device_id=target(dt, dl), device_id_type=MESH)
        guarded(dt, greet)

    tiles = [
        pltpu.make_async_copy(x_ref, xr.at[0, pl.ds(o, D), own, :], local.at[7]),
        pltpu.make_async_copy(y_ref, yr.at[:, own, :], local.at[8]),
        pltpu.make_async_copy(m_ref, mr.at[:, own, :], local.at[9]),
        pltpu.make_async_copy(land_ref, lr.at[own, :], local.at[10]),
    ]

    if n_t > 2:
        xr[...] = jnp.zeros_like(xr)
    for copy in tiles:
        copy.start()
    fetches = [
        pltpu.make_async_copy(a, b, local.at[i]) for i, (a, b) in enumerate(zip(weights, filled))
    ]
    for copy in fetches:
        copy.start()

    def src_lon(dl):
        return {-1: pl.ds(0, SIDE), 0: pl.ds(0, L), 1: pl.ds(L - SIDE, SIDE)}[dl]

    def own_lon(dl):
        lon = src_lon(dl)
        return pl.ds(SLOT + lon.start, lon.size)

    def dst_lon(dl):
        return {-1: pl.ds(SLOT + L, SIDE), 0: pl.ds(SLOT, L), 1: pl.ds(SLOT - SIDE, SIDE)}[dl]

    def x_copy(it, src, base_day, base_lon, dt, dl, index, sender):
        if dt == 2:
            first = (1 - sender) * (D - HALO_DAYS)
            goal = 0
        else:
            first = D - HALO_DAYS if dt == 1 else 0
            goal = window(sender + dt)
        days = D if dt == 0 else HALO_DAYS
        day = sender * D + first - goal
        lon = src_lon(dl)
        source = src.at[pl.ds(base_day + first, days), pl.ds(base_lon + lon.start, lon.size), :]
        return pltpu.make_async_remote_copy(
            src_ref=source,
            dst_ref=xr.at[it, pl.ds(day, days), dst_lon(dl), :],
            send_sem=send.at[index], recv_sem=recv.at[index],
            device_id=target(dt, dl), device_id_type=MESH,
        )

    def plain_copy(src, dst, dl, index):
        return pltpu.make_async_remote_copy(
            src_ref=src, dst_ref=dst, send_sem=send.at[index], recv_sem=recv.at[index],
            device_id=target(0, dl), device_id_type=MESH,
        )

    def x_start(it, src, base_day, base_lon, slot0):
        for i, (dt, dl) in enumerate(moves):
            def go(i=i, dt=dt, dl=dl):
                x_copy(it, src, base_day, base_lon, dt, dl, slot0 + i, t).start()
            guarded(dt, go)

    def x_wait(it, src, base_day, base_lon, slot0, straight):
        for i, (dt, dl) in enumerate(moves):
            if (dl == 0) != straight:
                continue
            def got(i=i, dt=dt, dl=dl):
                x_copy(it, src, base_day, base_lon, dt, dl, slot0 + i, group(dt, -1)).wait_recv()
            def sent(i=i, dt=dt, dl=dl):
                x_copy(it, src, base_day, base_lon, dt, dl, slot0 + i, t).wait_send()
            guarded(-dt, got)
            guarded(dt, sent)

    first_slot, next_slot, other_slot = 0, len(moves), 2 * len(moves)
    for copy in tiles:
        copy.wait()
    if pairs:
        around = 5
    else:
        around = 2 + 3 * ((t > 0).astype(jnp.int32) + (t < n_t - 1).astype(jnp.int32))
    pl.semaphore_wait(barrier, around)

    x_start(0, xr.at[0], o, SLOT, first_slot)
    others = []
    for i, dl in enumerate((-1, 1)):
        at = other_slot + 3 * i
        others.append(plain_copy(yr.at[:, own_lon(dl), :], yr.at[:, dst_lon(dl), :], dl, at))
        others.append(plain_copy(mr.at[:, own_lon(dl), :], mr.at[:, dst_lon(dl), :], dl, at + 1))
        others.append(plain_copy(lr.at[own_lon(dl), :], lr.at[dst_lon(dl), :], dl, at + 2))
    for copy in others:
        copy.start()

    for ref in (mh, ml):
        ref[...] = jnp.zeros_like(ref)
    for ref in (xh, xl, pb, qb):
        for day in (0, W + 1):
            ref[day] = jnp.zeros(ref.shape[1:], F32)
    if xh.shape[2] > R:
        for ref in (xh, xl):
            ref[:, :, R:, :] = jnp.zeros((W + 2, 3, xh.shape[2] - R, N), F32)
    h3[D * (L + 2) * 3 * S :, :] = jnp.zeros((h3.shape[0] - D * (L + 2) * 3 * S, N), BF16)
    ones = (iota((KG - 3 * GR, N), 0) < 3).astype(F32)
    for d in range(D):
        gf[d, 0 : 3 * GR, :] = jnp.zeros((3 * GR, N), F32)
        gf[d, 3 * GR :, :] = ones

    for copy in fetches:
        copy.wait()
    ew, dw = ew_ref[...], dw_ref[...]
    build_lift(ew, column(eb_ref[...]), te, False, turn)
    build_spread(dw, sd, False, turn)
    build_lift(dw, None, td, True, turn)
    build_spread(ew, se, True, turn)

    wide = gw_ref[...].astype(F32)
    gate_rows = iota((4 * S, 1), 0)
    scale = jnp.where((gate_rows >= 2 * S) & (gate_rows < 3 * S), 1.0, 0.5)
    wide = wide * scale
    gbias = column(gb_ref[...]) * scale
    b_hi = gbias.astype(BF16)
    b_rest = gbias - b_hi.astype(F32)
    b_mid = b_rest.astype(BF16).astype(F32)
    b_low = b_rest - b_mid
    ins = S + 1
    q = iota((4 * S, WG), 1)
    start = jnp.where(q == 3 * GR, b_hi.astype(F32), 0.0)
    start = jnp.where(q == 3 * GR + 1, b_mid, start)
    start = jnp.where(q == 3 * GR + 2, b_low, start)
    row = jnp.full((4 * S, WG), -1000, jnp.int32)
    taps = [jnp.zeros((4 * S, WG), F32) for _ in range(3)]
    for c in range(3):
        inside = (q >= c * GR) & (q < (c + 1) * GR)
        row = jnp.where(inside, q - c * GR, row)
        for b in range(3):
            k = (3 * b + c) * ins
            taps[b] = jnp.where(inside, wide[:, k : k + 1], taps[b])
    for j in range(L + 2):
        acc = start
        for b in range(3):
            acc = jnp.where(row == j + b, taps[b], acc)
        gwt[j] = acc.astype(BF16)

    for base in range(0, WS, 128):
        src = iota((9 * ins, 128), 0)
        lane = iota((9 * ins, 128), 1) + base
        want = lane + 1
        for i in range(1, 9):
            want = want + (lane >= i * S).astype(jnp.int32)
        pick = ((src == want) & (lane < 9 * S)).astype(F32).astype(BF16)
        wst[:, base : base + 128] = mm((0.5 * wide).astype(BF16), pick).astype(BF16)

    oweight = jnp.broadcast_to(0.5 * column(ow_ref[...]), (S, 2 * N))
    dbias = db_ref[0]

    def finish(parts):
        lower, mid, upper = parts
        lane = iota(lower.shape, 1)
        return (
            jnp.where(lane == 0, 0.0, pltpu.roll(lower, 1, 1))
            + mid
            + jnp.where(lane == N - 1, 0.0, pltpu.roll(upper, N - 1, 1))
        )

    def gather_taps(ref, d, i):
        parts = []
        for c in range(3):
            rows = [pl.ds((3 * a + c) * BLOCK, BLOCK) for a in range(3)]
            parts.append(ref[d, i, rows[0], :] + ref[d + 1, i, rows[1], :] + ref[d + 2, i, rows[2], :])
        return finish(parts)

    def planes(ref, d, n, rows):
        return [
            jnp.concatenate([ref[d + a + q, c, rows, :] for q in range(n)], axis=1)
            for a in range(3)
            for c in range(3)
        ]

    def span(radius):
        n = D + radius if pairs else min(W, D + 2 * radius)
        n = min(W, n)
        return (0 if pairs or n == W else jnp.clip(o - radius, 0, W - n)), n

    def groups(start, n):
        return [(start + k, min(2, n - k)) for k in range(0, n, 2)]

    def spread(weight, hidden, rest, size, count, out, d, n):
        rows = weight.shape[0] // 2
        for i in range(count):
            at = slice(i * BLOCK * C, min((i * BLOCK + SLAB) * C, size))
            k = at.stop - at.start
            sums = mm(weight[:, 0:k], hidden(at))
            sums = sums[0:rows] + sums[rows:] + mm(weight[0 : up(rows, 16), 0:k], rest(at))[0:rows]
            for q in range(n):
                out[d + q + 1, i] = sums[:, q * N : (q + 1) * N]

    def lift(weight, hi_ref, lo_ref, d, n, first, extra):
        rows = pl.ds(first, SLAB)
        hi = jnp.concatenate(planes(hi_ref, d, n, rows) + [extra[:, 0 : n * N]], axis=0).astype(BF16)
        lo = jnp.concatenate(planes(lo_ref, d, n, rows) + [blank[:, 0 : n * N]], axis=0).astype(BF16)
        pad = jnp.zeros((weight.shape[1] - 30 * SLAB, n * N), BF16)
        return mm(weight, jnp.concatenate([hi, lo, hi, pad], axis=0))

    unit = (iota((SLAB, 2 * N), 0) == 0).astype(F32)
    blank = jnp.zeros((SLAB, 2 * N), F32)

    s3, n3 = span(3)
    early = [i for i in range(NB) if BLOCK * i >= 6 and BLOCK * i + SLAB <= L + 6]
    late = [i for i in range(NB) if i not in early]

    def stage(it, first, rows):
        at = pl.ds(first, rows)
        for d in range(W):
            for c, v in enumerate(shifts(xr[it, actual(d), at, :])):
                hi = v.astype(BF16).astype(F32)
                xh[d + 1, c, at, :] = hi
                xl[d + 1, c, at, :] = v - hi

    def encode(blocks):
        for d, n in groups(s3, n3):
            for i in blocks:
                enc = jnp.maximum(lift(te[...], xh, xl, d, n, SLOT - 6 + BLOCK * i, unit), 0.0)
                to = pl.ds(BLOCK * C * i, BLOCK * C)
                for ref, v in zip((hid, rem), halves(enc)):
                    for q in range(n):
                        ref[d + q, to, :] = v[:, q * N : (q + 1) * N]

    def begin(it):
        stage(it, SLOT, L)
        encode(early)

    def joined(ref, d, n):
        return lambda at: jnp.concatenate([ref[d + q, at, :] for q in range(n)], axis=1)

    def gradient(it):
        stage(it, 0, SLOT)
        stage(it, SLOT + L, SLOT)
        encode(late)
        for d, n in groups(s3, n3):
            spread(sd, joined(hid, d, n), joined(rem, d, n), NB * BLOCK * C, MB, pb, d, n)

        s2, n2 = span(2)
        for k in range(n2):
            d = s2 + k
            for i in range(MB):
                at = pl.ds(SLOT - 4 + BLOCK * i, BLOCK)
                rebuilt = gather_taps(pb, d, i) + dbias
                mis = lr[at, :].astype(F32) * (xr[it, actual(d), at, :] - rebuilt)
                to = pl.ds(BLOCK * i, BLOCK)
                mis_ref[d, to, :] = mis
                for c, v in enumerate(shifts(mis)):
                    hi = v.astype(BF16).astype(F32)
                    mh[d + 1, c, to, :] = hi
                    ml[d + 1, c, to, :] = v - hi

        s1, n1 = span(1)
        for d, n in groups(s1, n1):
            on = joined(hid, d, n)
            for i in range(-(-BH // BLOCK)):
                count = min(BLOCK, BH - BLOCK * i) * C
                lifted = lift(td[0:count, :], mh, ml, d, n, BLOCK * i, blank)
                at = (2 + BLOCK * i) * C
                live = on(slice(at, at + count)) > jnp.zeros((), BF16)
                for ref, v in zip((bid, bem), halves(lifted)):
                    v = jnp.where(live, v, jnp.zeros((), BF16))
                    for q in range(n):
                        ref[d + q, BLOCK * C * i : BLOCK * C * i + count, :] = v[:, q * N : (q + 1) * N]
        for d, n in groups(s1, n1):
            spread(se, joined(bid, d, n), joined(bem, d, n), BH * C, GB, qb, d, n)

        for k in range(D):
            d = home + k
            for i in range(GB):
                at = pl.ds(SLOT - 2 + BLOCK * i, BLOCK)
                seen = mr[mine(k), at, :].astype(F32)
                grad = (
                    2.0 * seen * (xr[it, actual(d), at, :] - yr[mine(k), at, :])
                    + mis_ref[d, pl.ds(2 + BLOCK * i, BLOCK), :]
                    - gather_taps(qb, d, i)
                )
                for c, v in enumerate(shifts(grad)):
                    gf[k, pl.ds(c * GR + BLOCK * i, BLOCK), :] = v
        for p in range(HALF):
            v = jnp.concatenate([gf[2 * p], gf[2 * p + 1]], axis=1).astype(BF16)
            g3[p, 0:KG, :] = v
            if WG > KG:
                g3[p, KG:, :] = jnp.zeros((WG - KG, 2 * N), BF16)

    def twice(v):
        return jnp.tanh(v) + 1.0

    def put_h3(d, lon, h):
        v = jnp.concatenate(list(shifts(h)), axis=0).astype(BF16)
        h3[pl.ds(pl.multiple_of((d * (L + 2) + lon) * 3 * S, 16), 3 * S), :] = v

    x_wait(0, xr.at[0], o, SLOT, first_slot, True)
    begin(0)
    for copy in others:
        copy.wait()
    x_wait(0, xr.at[0], o, SLOT, first_slot, False)
    gradient(0)

    def first_gates(j, inside):
        for p in range(HALF):
            rhs = g3[p]
            up_ = mm(gwt[j, 0:S, :], rhs)
            rest = mm(gwt[j, 2 * S : 4 * S, :], rhs)
            state = 0.5 * (twice(up_) * jnp.tanh(rest[0:S]))
            hidden = twice(rest[S : 2 * S]) * jnp.tanh(state)
            if inside:
                cell[j - 1, p] = state
                step = jnp.sum(oweight * hidden, axis=0, keepdims=True)
            for i in range(2):
                d = 2 * p + i
                hraw[d, j] = hidden[:, i * N : (i + 1) * N]
                if inside:
                    at = pl.ds(SLOT - 1 + j, 1)
                    to = actual(home + d)
                    xr[1, to, at, :] = xr[0, to, at, :] - step[:, i * N : (i + 1) * N]

    def inner(j, carry):
        first_gates(j, True)
        return carry

    lax.fori_loop(1, L + 1, inner, 0, unroll=8)
    x_start(1, xr.at[1], o, SLOT, next_slot)
    first_gates(0, False)
    first_gates(L + 1, False)

    def place(j, carry):
        for d in range(D):
            put_h3(d, j, hraw[d, j])
        return carry

    lax.fori_loop(0, L + 2, place, 0, unroll=2)

    def state_part(j, carry):
        for p in range(HALF):
            rhs = jnp.concatenate(
                [
                    h3[pl.ds(pl.multiple_of(((2 * p + i) * (L + 2) + j) * 3 * S, 16), WS), :]
                    for i in range(2)
                ],
                axis=1,
            )
            gst[j, p] = mm(wst[...], rhs)
        return carry

    lax.fori_loop(0, L, state_part, 0, unroll=2)
    x_wait(1, xr.at[1], o, SLOT, next_slot, True)
    begin(1)
    x_wait(1, xr.at[1], o, SLOT, next_slot, False)
    gradient(1)

    def last_gates(j, carry):
        for p in range(HALF):
            sums = gst[j, p] + mm(gwt[j + 1], g3[p])
            state = twice(sums[S : 2 * S]) * cell[j, p] + twice(sums[0:S]) * jnp.tanh(
                sums[2 * S : 3 * S]
            )
            hidden = twice(sums[3 * S :]) * jnp.tanh(0.5 * state)
            step = jnp.sum(oweight * hidden, axis=0, keepdims=True)
            for i in range(2):
                d = 2 * p + i
                out_ref[mine(d), pl.ds(j, 1), :] = (
                    xr[1, actual(home + d), pl.ds(SLOT + j, 1), :] - step[:, i * N : (i + 1) * N]
                )
        return carry

    lax.fori_loop(0, L, last_gates, 0, unroll=8)


def body(n_t, n_l, x, y, m, land, ew, eb, dw, db, gw, gb, ow):
    D, L, N = x.shape[1:]
    C = eb.shape[0]
    S = ow.shape[0]
    R = L + 2 * SLOT
    NB, MB, GB, BH, MR, GR = sizes(L)
    W = min(n_t * D, D + 2 * HALO_DAYS)
    RX = max(R, up(BLOCK * NB + 4, 8))
    RM = up(max(BLOCK * MB, BLOCK * (-(-BH // BLOCK) - 1) + SLAB), 8)
    taps = up(9 * BLOCK, 8)
    KG = up(3 * GR + 3, 16)
    WE, WG, WS = up(30 * SLAB, 128), KG, up(9 * S, 128)
    G = 4 * S
    copies = 2 * (5 if n_t == 2 else 8) + 6
    vm = pltpu.VMEM
    scratch = [
        vm((2, W, R, N), F32), vm((D, R, N), F32), vm((D, R, N), jnp.int32), vm((R, N), jnp.int32),
        vm((W + 2, 3, RX, N), F32), vm((W + 2, 3, RX, N), F32),
        vm((W + 2, 3, RM, N), F32), vm((W + 2, 3, RM, N), F32),
        vm((W, NB * BLOCK * C, N), BF16), vm((W, NB * BLOCK * C, N), BF16),
        vm((W, BH * C, N), BF16), vm((W, BH * C, N), BF16), vm((W + 2, MB, taps, N), F32), vm((W + 2, GB, taps, N), F32),
        vm((W, RM, N), F32), vm((D, KG, N), F32), vm((D // 2, WG, 2 * N), BF16), vm((D, L + 2, S, N), F32),
        vm((D * (L + 2) * 3 * S + WS - 9 * S, N), BF16), vm((L, D // 2, S, 2 * N), F32),
        vm((BLOCK * C, WE), BF16), vm((BLOCK * C, WE), BF16),
        vm((2 * taps, SLAB * C), BF16), vm((2 * taps, SLAB * C), BF16),
        vm((L + 2, G, WG), BF16), vm((G, WS), BF16), vm((L, D // 2, G, 2 * N), F32),
        pltpu.SemaphoreType.DMA((copies,)), pltpu.SemaphoreType.DMA((copies,)),
        pltpu.SemaphoreType.DMA((11,)),
    ]
    v = pl.BlockSpec(memory_space=pltpu.VMEM)
    whole = pl.BlockSpec(memory_space=pltpu.HBM)
    weights = (ew, eb[None], dw, db, gw, gb[None], ow[None])
    scratch = [(pltpu.SMEM if w is db else vm)(w.shape, w.dtype) for w in weights] + scratch
    out = pl.pallas_call(
        functools.partial(kernel, n_t, n_l, D, L, C, S),
        out_shape=pltpu.VMEM((D, L, N), F32),
        in_specs=[whole] * 11,
        out_specs=v,
        scratch_shapes=scratch,
        compiler_params=pltpu.CompilerParams(
            collective_id=0, has_side_effects=True, vmem_limit_bytes=67000000
        ),
        name="solver",
    )(x[0], y[0], m[0], land, *weights)
    return out[None]


def solution(mesh):
    tile = P(None, "tm", "lon", None)
    run = functools.partial(body, mesh.shape["tm"], mesh.shape["lon"])
    return jax.shard_map(
        run, mesh=mesh, in_specs=(tile, tile, tile, P("lon", None)) + (P(),) * 7,
        out_specs=tile, check_vma=False,
    )
```
